512 devices in a mesh: freq: 128 (over x, z, core), bl: 4 (over y).
Axes of the slice: x: 4, y: 4, z: 16, core: 2. Of those that a mesh axis runs over, the one named last changes fastest.
Arguments:
- vis_time: bfloat16 [128, 2, 1024, 2048], P('freq', None, 'bl'), may hold values from -6 to 6
- owner: int32 [384, 1], replicated, may hold values from 0 to 127; in each aligned block of 384 rows (0 to 383, 384 to 767, ...) at most 4 rows name the same one
- counts: int32 [384, 128], replicated, may hold values from 1 to 4
- factors: bfloat16 [512, 128, 2, 4, 1024], P('freq', None, None, None, 'bl'), may hold values from -0.1875 to 0.1875
Outputs:
- filtered: bfloat16 [128, 2, 1024, 384], P('freq', None, 'bl')
The draws below stay inside these ranges and needn't reach their ends.
Inputs may be any that keep to these rules, and one draw needn't show every extreme that they name: `owner`: every index of freq owns at least one m and at most 4; some index owns exactly 4.
All inputs are finite; a program needn't handle non-finite values.
Results may differ from the reference program's by a relative error of at most 0.0064.
Values may be sent and summed in bfloat16 or wider, within the bound.
No kernel may reach another device: no remote copies, remote signals or barrier semaphores. Data moves between devices by JAX's collectives and lax.ppermute only.
A program may use at most 64 MiB of HBM per device.

```python
import math
import jax
import jax.numpy as jnp
import numpy as np
from jax import lax

NB = 1024
NT = 2048
K = 4
NF = 128
MM = 384
CAP = 4
SLOTS = 512
N_FREQ = 128


def touch_ends(result, stream_key, low, high):
    longest = result.shape.index(max(result.shape))
    spots = []
    for shift in (0, 1):
        where = [jax.random.randint(jax.random.fold_in(stream_key, axis), (), 0, length) for axis, length in enumerate(result.shape)]
        where[longest] = (where[longest] + shift) % result.shape[longest]
        spots.append(tuple(where))
    return result.at[spots[0]].set(low).at[spots[1]].set(high)


def level_of(stream_key, extent, pieces, low, high):
    loudness, own = 1.0, jax.random.fold_in(stream_key, 6)
    for position, parts in pieces:
        draws = jnp.exp(jax.random.uniform(jax.random.fold_in(own, position), (parts,), jnp.float32, low / len(pieces), high / len(pieces)))
        loudness = loudness * jnp.repeat(draws, extent[position] // parts).reshape([-1 if axis == position else 1 for axis in range(len(extent))])
    return loudness


def shared_out(stream_key, own, number, rows, amount, top, reach, lean):
    sequence = jax.random.permutation(stream_key, amount)
    heavy_load, common = load_shares(amount, rows * top, reach, lean, True), load_shares(amount, rows * top, reach, lean, False)
    places = jnp.arange(amount)

    def named(tallies, turn):
        used = int((tallies > 0).sum())
        fixed = max(1, used // 4)
        shifted = fixed + (places - fixed + turn * (used - fixed)) % max(1, amount - fixed)
        return jnp.zeros((amount,), jnp.int32).at[sequence[jnp.where(places < fixed, places, shifted)]].set(jnp.asarray(tallies, jnp.int32))

    tallies = jnp.where(number % 4 == 0, named(heavy_load, number // 4), named(common, number - number // 4 - 1))
    mixed = jax.random.permutation(jax.random.fold_in(own, 3), amount)
    giver, receiver = mixed[0:amount // 2 * 2:2], mixed[1:amount // 2 * 2:2]
    slack = jnp.minimum(tallies[giver] - 1, reach - tallies[receiver]) // 2
    slack = jnp.where((giver == sequence[0]) | (receiver == sequence[0]) | (tallies[receiver] == 0), 0, jnp.maximum(slack, 0))
    shifted = jax.random.randint(jax.random.fold_in(own, 4), (amount // 2,), 0, 1 << 20) % (slack + 1)
    tallies = tallies.at[giver].add(-shifted).at[receiver].add(shifted)
    members = jnp.searchsorted(jnp.cumsum(tallies), jnp.arange(rows * top), side="right").astype(jnp.int32)
    listing = members.reshape(top, rows).T
    listing = listing[jax.random.permutation(jax.random.fold_in(own, 1), rows)]
    turn = jax.random.randint(jax.random.fold_in(own, 2), (rows, 1), 0, top)
    return jnp.take_along_axis(listing, (jnp.arange(top)[None, :] + turn) % top, axis=1)


def load_shares(amount, total, bound, slope, full):
    loads = [(1 << 20) // math.isqrt(standing ** slope) + 1 for standing in range(1, amount + 1)]
    largest = bound if full else min(bound, max(-(-total // amount), total * loads[0] // sum(loads)))
    least = 1 if total - largest >= amount - 1 else 0
    holding, surplus = [largest] + [least] * (amount - 1), total - largest - least * (amount - 1)
    while surplus > 0:
        free = [i for i in range(1, amount) if holding[i] < largest] or [i for i in range(1, amount) if holding[i] < bound]
        mass, remaining = sum([loads[i] for i in free]), surplus
        for i in free:
            addition = min(bound - holding[i], max(1, remaining * loads[i] // mass), surplus)
            holding[i] = holding[i] + addition
            surplus = surplus - addition
    return np.array(holding)


def gaussian(own_key, shape, deviation, limit, shards=(), kind=jnp.bfloat16):
    drawn = deviation * jax.random.normal(own_key, shape, jnp.float32)
    if shards:
        drawn = drawn * level_of(own_key, shape, shards, -0.22, 0.18)
    return jnp.clip(drawn, -limit, limit).astype(kind)


def setup_inputs(seed: int = 0) -> dict:
    arg_keys = jax.random.split(jax.random.key(seed), 5)
    vis_time = gaussian(arg_keys[0], (NF, 2, NB, NT), 1.0, 6.0, ((0, 128), (2, 4)))
    owner_keys = jax.random.split(jax.random.fold_in(arg_keys[1], 1), MM // MM)
    owner_turns = jax.random.permutation(jax.random.fold_in(arg_keys[1], 3), MM // MM)
    owner = jax.vmap(lambda own, number: shared_out(jax.random.fold_in(arg_keys[1], 2), own, number, MM, N_FREQ, 1, CAP, 2))(owner_keys, owner_turns).reshape((MM, 1))
    counts = touch_ends(jax.random.randint(arg_keys[2], (MM, NF), 1, K + 1), jax.random.fold_in(arg_keys[2], 1), 1, K).astype(jnp.int32)
    factors = gaussian(arg_keys[3], (SLOTS, NF, 2, K, NB), NB ** -0.5, 0.1875, ((0, 128), (4, 4)))
    return {"vis_time": vis_time, "owner": owner, "counts": counts, "factors": factors}


def wave_tables(columns, samples):
    times = jnp.arange(samples, dtype=jnp.int32)
    phases = times[:, None] * columns[None, :] % samples
    angles = phases.astype(jnp.float32) * (2.0 * math.pi / samples)
    factor_scale = 1.0 / math.sqrt(samples)
    return jnp.concatenate([jnp.cos(angles) * factor_scale, jnp.sin(angles) * factor_scale], axis=1).astype(jnp.bfloat16)

def reference(vis_time, owner, counts, factors):
    owners_of = owner[:, 0]
    owner_ids = jnp.arange(N_FREQ, dtype=jnp.int32)
    onehot = (owners_of[:, None] == owner_ids[None, :]).astype(jnp.int32)
    before = jnp.cumsum(onehot, axis=0) - onehot
    ranking = lax.optimization_barrier(jnp.sum(before * onehot, axis=1))
    slot_of = (owners_of * CAP + ranking).astype(jnp.int32)
    wave_table = wave_tables(jnp.arange(MM, dtype=jnp.int32), NT)
    flattened = vis_time.reshape(NF * 2 * NB, NT)
    spectra = jnp.dot(flattened, wave_table, preferred_element_type=jnp.float32).reshape(NF, 2, NB, 2, MM)
    real_part = spectra[:, 0, :, 0] + spectra[:, 1, :, 1]
    imag_part = spectra[:, 1, :, 0] - spectra[:, 0, :, 1]
    m_modes = jnp.stack([real_part, imag_part], axis=1).astype(jnp.bfloat16)
    factor_scale = math.sqrt(NB / K)
    rank_ids = jnp.arange(K, dtype=jnp.int32)

    def one_mode(mode_index):
        slot_index = slot_of[mode_index]
        factor = lax.dynamic_index_in_dim(factors, slot_index, 0, keepdims=False).astype(jnp.float32)
        m_column = lax.dynamic_index_in_dim(m_modes, mode_index, 3, keepdims=False).astype(jnp.float32)
        fac_re, fac_im = (factor[:, 0], factor[:, 1])
        vis_re, vis_im = (m_column[:, 0], m_column[:, 1])
        coef_re = jnp.einsum('fkb,fb->fk', fac_re, vis_re) + jnp.einsum('fkb,fb->fk', fac_im, vis_im)
        coef_im = jnp.einsum('fkb,fb->fk', fac_re, vis_im) - jnp.einsum('fkb,fb->fk', fac_im, vis_re)
        limits = lax.dynamic_index_in_dim(counts, mode_index, 0, keepdims=False)
        retained = rank_ids[None, :] < limits[:, None]
        kept_re = jnp.where(retained, coef_re, 0.0).astype(jnp.bfloat16)
        kept_im = jnp.where(retained, coef_im, 0.0).astype(jnp.bfloat16)
        kept_re, kept_im = lax.optimization_barrier((kept_re, kept_im))
        kept_re = kept_re.astype(jnp.float32)
        kept_im = kept_im.astype(jnp.float32)
        syn_re = (jnp.einsum('fkb,fk->fb', fac_re, kept_re) - jnp.einsum('fkb,fk->fb', fac_im, kept_im)) * factor_scale
        syn_im = (jnp.einsum('fkb,fk->fb', fac_re, kept_im) + jnp.einsum('fkb,fk->fb', fac_im, kept_re)) * factor_scale
        return jnp.stack([syn_re, syn_im], axis=1).astype(jnp.bfloat16)
    synthesis = lax.map(one_mode, jnp.arange(MM, dtype=jnp.int32))
    return jnp.transpose(synthesis, (1, 2, 3, 0))
```

```python
import math

import jax
import jax.numpy as jnp
import numpy as np
from jax import lax
from jax.experimental import pallas as pl
from jax.experimental.pallas import tpu as pltpu
from jax.sharding import PartitionSpec as P

NB = 1024
NT = 2048
K = 4
MM = 384
CAP = 4
STEPS = 4
F32 = jnp.float32
BF16 = jnp.bfloat16


def wave_rows():
    phases = np.outer(np.arange(MM), np.arange(NT)) % NT
    angles = phases * (2.0 * math.pi / NT)
    rows = np.concatenate([np.cos(angles), np.sin(angles)], axis=0) / math.sqrt(NT)
    return rows.astype(np.float32).astype(jnp.bfloat16)


def dft_kernel(owner_ref, vis_ref, wave_ref, out_ref, target_ref, acc_ref):
    step = pl.program_id(0)
    owners = out_ref.shape[0] // (2 * CAP)

    @pl.when(step == 0)
    def _():
        acc_ref[...] = jnp.zeros_like(acc_ref)
        hot = owner_ref[...] == lax.broadcasted_iota(jnp.int32, (owners, MM), 0)
        hot = jnp.where(hot, 1.0, 0.0)
        earlier = lax.broadcasted_iota(jnp.int32, (MM, MM), 0) < lax.broadcasted_iota(
            jnp.int32, (MM, MM), 1
        )
        earlier = jnp.where(earlier, 1.0, 0.0).astype(BF16)
        before = jnp.dot(hot.astype(BF16), earlier, preferred_element_type=F32)
        rank = jnp.sum(before * hot, axis=0, keepdims=True).astype(jnp.int32)
        target_ref[...] = owner_ref[...] * (2 * CAP) + rank

    acc_ref[...] += lax.dot_general(
        wave_ref[...], vis_ref[...], (((1,), (1,)), ((), ())), preferred_element_type=F32
    )

    @pl.when(step == pl.num_programs(0) - 1)
    def _():
        half = acc_ref.shape[1] // 2
        real = acc_ref[:MM, :half] + acc_ref[MM:, half:]
        imag = acc_ref[:MM, half:] - acc_ref[MM:, :half]
        modes = jnp.concatenate([real, imag], axis=0).astype(BF16)
        target = target_ref[...]
        target = jnp.concatenate([target, target + CAP], axis=1)
        rows = lax.broadcasted_iota(jnp.int32, (out_ref.shape[0], 2 * MM), 0)
        placing = jnp.where(rows == target, 1.0, 0.0).astype(BF16)
        out_ref[...] = jnp.dot(placing, modes, preferred_element_type=F32).astype(BF16)


def coef_kernel(vis_ref, fac_ref, out_ref):
    freqs, _, base = vis_ref.shape
    top = lax.broadcasted_iota(jnp.int32, (1, 2 * CAP, base), 1) < CAP
    lanes = lax.broadcasted_iota(jnp.int32, (2 * CAP, freqs), 1)
    block = 8

    def body(i, acc):
        first = pl.multiple_of(i * block, block)
        vis = vis_ref[pl.ds(first, block)].astype(F32)
        swapped = pltpu.roll(vis, CAP, 1)
        vis_re = jnp.where(top, vis, swapped)
        vis_im = jnp.where(top, swapped, vis)
        sums = []
        for pair in range(K // 2):
            fac_re = fac_ref[pl.ds(first, block), pl.ds(pair * 8, 8)].astype(F32)
            fac_im = fac_ref[pl.ds(first, block), pl.ds(16 + pair * 8, 8)].astype(F32)
            re = fac_re * vis_re + fac_im * vis_im
            im = fac_re * vis_im - fac_im * vis_re
            sums.append((jnp.sum(re, axis=2, keepdims=True), jnp.sum(im, axis=2, keepdims=True)))
        acc = list(acc)
        for j in range(block):
            here = lanes == first + j
            for ri in range(2):
                for pair in range(K // 2):
                    at = ri * 2 + pair
                    acc[at] = jnp.where(here, sums[pair][ri][j], acc[at])
        return tuple(acc)

    zero = jnp.zeros((2 * CAP, freqs), F32)
    acc = lax.fori_loop(0, freqs // block, body, (zero,) * 4)
    for at in range(4):
        for copy in range(out_ref.shape[0]):
            out_ref[copy, pl.ds(at * 8, 8), :] = acc[at]


def synth_kernel(part_ref, keep_ref, fac_ref, out_ref):
    freqs, _, base = out_ref.shape
    block = 8
    total = part_ref[0]
    for source in range(1, part_ref.shape[0]):
        total = total + part_ref[source]
    keep = keep_ref[...]
    keep = jnp.concatenate([keep, keep], axis=0)
    kept = jnp.where(keep > 0, total, 0.0).astype(BF16).astype(F32)
    kept = kept * math.sqrt(NB / K)
    top = lax.broadcasted_iota(jnp.int32, (2 * CAP, base), 0) < CAP

    def body(i, kept):
        first = pl.multiple_of(i * block, block)
        for j in range(block):
            re = jnp.zeros((2 * CAP, base), F32)
            im = jnp.zeros((2 * CAP, base), F32)
            for pair in range(K // 2):
                fac_re = fac_ref[first + j, pl.ds(pair * 8, 8)].astype(F32)
                fac_im = fac_ref[first + j, pl.ds(16 + pair * 8, 8)].astype(F32)
                kept_re = kept[pair * 8 : pair * 8 + 8, j : j + 1]
                kept_im = kept[16 + pair * 8 : 24 + pair * 8, j : j + 1]
                re = re + (fac_re * kept_re - fac_im * kept_im)
                im = im + (fac_re * kept_im + fac_im * kept_re)
            re = re + pltpu.roll(re, CAP, 0)
            im = im + pltpu.roll(im, CAP, 0)
            out_ref[first + j] = jnp.where(top, re, im).astype(BF16)
        return pltpu.roll(kept, freqs - block, 1)

    lax.fori_loop(0, freqs // block, body, kept)


def final_kernel(target_ref, slots_ref, out_ref):
    rows = lax.broadcasted_iota(jnp.int32, (slots_ref.shape[0], MM), 0)
    for part in range(2):
        placing = jnp.where(rows == target_ref[...] + part * CAP, 1.0, 0.0).astype(BF16)
        out_ref[part] = lax.dot_general(
            slots_ref[...], placing, (((0,), (0,)), ((), ())), preferred_element_type=F32
        ).astype(BF16)


def local(vis_time, owner, counts, factors):
    n_freq = lax.axis_size("freq")
    n_bl = lax.axis_size("bl")
    myself = lax.axis_index("freq")
    base = vis_time.shape[2]
    flat = vis_time.reshape(2 * base, NT)
    owner_row = owner.reshape(1, MM)
    width = 2 * CAP
    outgoing, target = pl.pallas_call(
        dft_kernel,
        grid=(STEPS,),
        in_specs=[
            pl.BlockSpec((1, MM), lambda i: (0, 0)),
            pl.BlockSpec((2 * base, NT // STEPS), lambda i: (0, i)),
            pl.BlockSpec((2 * MM, NT // STEPS), lambda i: (0, i)),
        ],
        out_specs=[
            pl.BlockSpec((n_freq * width, base), lambda i: (0, 0)),
            pl.BlockSpec((1, MM), lambda i: (0, 0)),
        ],
        out_shape=[
            jax.ShapeDtypeStruct((n_freq * width, base), BF16),
            jax.ShapeDtypeStruct((1, MM), jnp.int32),
        ],
        scratch_shapes=[pltpu.VMEM((2 * MM, 2 * base), F32)],
        compiler_params=pltpu.CompilerParams(vmem_limit_bytes=40 << 20),
        name="dft",
    )(owner_row, flat, jnp.asarray(wave_rows()))
    incoming = lax.all_to_all(
        outgoing.reshape(n_freq, width, base), "freq", split_axis=0, concat_axis=0, tiled=True
    )

    slot_rows = myself * width + jnp.arange(CAP, dtype=jnp.int32)
    mine = (target == slot_rows[:, None]).astype(BF16)
    limits = jnp.dot(mine, counts.astype(BF16), preferred_element_type=F32)
    keep = jnp.arange(K, dtype=F32)[:, None, None] < limits[None]
    keep = keep.astype(F32).reshape(K * CAP, n_freq)
    by_freq = jnp.transpose(factors, (1, 2, 3, 0, 4)).reshape(n_freq, 2 * K * CAP, base)

    partial = pl.pallas_call(
        coef_kernel,
        out_shape=jax.ShapeDtypeStruct((n_bl, 2 * K * CAP, n_freq), F32),
        compiler_params=pltpu.CompilerParams(vmem_limit_bytes=40 << 20),
        name="coef",
    )(incoming, by_freq)
    partials = lax.all_to_all(partial, "bl", split_axis=0, concat_axis=0, tiled=True)
    synthesis = pl.pallas_call(
        synth_kernel,
        out_shape=jax.ShapeDtypeStruct((n_freq, width, base), BF16),
        compiler_params=pltpu.CompilerParams(vmem_limit_bytes=40 << 20),
        name="synth",
    )(partials, keep, by_freq)
    returned = lax.all_to_all(synthesis, "freq", split_axis=0, concat_axis=0, tiled=True)
    filtered = pl.pallas_call(
        final_kernel,
        out_shape=jax.ShapeDtypeStruct((2, base, MM), BF16),
        compiler_params=pltpu.CompilerParams(vmem_limit_bytes=40 << 20),
        name="final",
    )(target, returned.reshape(n_freq * width, base))
    return filtered[None]


def solution(mesh):
    placed = (P("freq", None, "bl", None), P(), P(), P("freq", None, None, None, "bl"))
    return jax.shard_map(
        local, mesh=mesh, in_specs=placed, out_specs=P("freq", None, "bl", None), check_vma=False
    )
```

```python
import math

import jax
import jax.numpy as jnp
import numpy as np
from jax import lax
from jax.experimental import pallas as pl
from jax.experimental.pallas import tpu as pltpu
from jax.sharding import PartitionSpec as P

NB = 1024
NT = 2048
K = 4
MM = 384
CAP = 4
CHUNK = NT // 4
BLOCK = 32
F32 = jnp.float32
BF16 = jnp.bfloat16


def wave_half():
    phases = np.outer(np.arange(NT // 2), np.arange(MM)) % NT
    angles = phases * (2.0 * math.pi / NT)
    rows = np.concatenate([np.cos(angles), np.sin(angles)], axis=1) / math.sqrt(NT)
    return rows.astype(np.float32).astype(jnp.bfloat16)


def dft_kernel(owner_hbm, vis_hbm, wave_hbm, out_ref, target_ref, owner_ref, vis_ref, wave_ref, sems):
    owners = out_ref.shape[0] // (2 * CAP)
    owner_copy = pltpu.make_async_copy(owner_hbm, owner_ref, sems.at[0])
    owner_copy.start()
    wave_copies, vis_copies = [], {}
    for part in range(2):
        wave_copies.append(
            pltpu.make_async_copy(
                wave_hbm.at[pl.ds(part * CHUNK, CHUNK)], wave_ref.at[part], sems.at[1 + part]
            )
        )
        wave_copies[-1].start()
        for chunk in (part, part + 2):
            vis_copies[chunk] = pltpu.make_async_copy(
                vis_hbm.at[:, pl.ds(chunk * CHUNK, CHUNK)], vis_ref.at[chunk], sems.at[3 + chunk]
            )
            vis_copies[chunk].start()
    owner_copy.wait()
    owner = owner_ref[...]
    hot = owner == lax.broadcasted_iota(jnp.int32, (owners, MM), 0)
    hot = jnp.where(hot, 1.0, 0.0)
    earlier = lax.broadcasted_iota(jnp.int32, (MM, MM), 0) < lax.broadcasted_iota(
        jnp.int32, (MM, MM), 1
    )
    earlier = jnp.where(earlier, 1.0, 0.0).astype(BF16)
    before = jnp.dot(hot.astype(BF16), earlier, preferred_element_type=F32)
    rank = jnp.sum(before * hot, axis=0, keepdims=True).astype(jnp.int32)
    target = owner * (2 * CAP) + rank
    target_ref[...] = target
    target = jnp.concatenate([target, target + CAP], axis=1)
    rows = lax.broadcasted_iota(jnp.int32, (out_ref.shape[0], 2 * MM), 0)
    placing = jnp.where(rows == target, 1.0, 0.0).astype(BF16)

    sign = 1 - 2 * (lax.broadcasted_iota(jnp.int32, (1, 2 * MM), 1) % 2)
    sign = sign.astype(F32)
    spectra = None
    for part in range(2):
        wave_copies[part].wait()
        for half in range(2):
            chunk = part + 2 * half
            vis_copies[chunk].wait()
            product = jnp.dot(vis_ref[chunk], wave_ref[part], preferred_element_type=F32)
            if half == 1:
                product = product * sign
            spectra = product if spectra is None else spectra + product
    base = spectra.shape[0] // 2
    real = spectra[:base, :MM] + spectra[base:, MM:]
    imag = spectra[base:, :MM] - spectra[:base, MM:]
    modes = jnp.concatenate([real, imag], axis=1).astype(BF16)
    out_ref[...] = lax.dot_general(
        placing, modes, (((1,), (1,)), ((), ())), preferred_element_type=F32
    ).astype(BF16)


def coef_kernel(vis_ref, fac_ref, limit_ref, out_ref, keep_ref):
    freqs, _, base = vis_ref.shape
    top = lax.broadcasted_iota(jnp.int32, (1, 2 * CAP, base), 1) < CAP
    lanes = lax.broadcasted_iota(jnp.int32, (2 * CAP, freqs), 1)
    block = BLOCK
    ranks = lax.broadcasted_iota(jnp.int32, (2 * K * CAP, freqs), 0) // CAP % K
    limits = jnp.concatenate([limit_ref[...]] * (2 * K), axis=0)
    keep_ref[...] = jnp.where(ranks.astype(F32) < limits, 1.0, 0.0)

    def body(i, acc):
        first = pl.multiple_of(i * block, block)
        vis = vis_ref[pl.ds(first, block)].astype(F32)
        swapped = pltpu.roll(vis, CAP, 1)
        vis_re = jnp.where(top, vis, swapped)
        vis_im = jnp.where(top, swapped, vis)
        sums = []
        for pair in range(K // 2):
            fac_re = fac_ref[pl.ds(first, block), pl.ds(pair * 8, 8)].astype(F32)
            fac_im = fac_ref[pl.ds(first, block), pl.ds(16 + pair * 8, 8)].astype(F32)
            re = fac_re * vis_re + fac_im * vis_im
            im = fac_re * vis_im - fac_im * vis_re
            sums.append((jnp.sum(re, axis=2, keepdims=True), jnp.sum(im, axis=2, keepdims=True)))
        acc = list(acc)
        for j in range(block):
            here = lanes == first + j
            for ri in range(2):
                for pair in range(K // 2):
                    at = ri * 2 + pair
                    acc[at] = jnp.where(here, sums[pair][ri][j], acc[at])
        return tuple(acc)

    zero = jnp.zeros((2 * CAP, freqs), F32)
    acc = lax.fori_loop(0, freqs // block, body, (zero,) * 4)
    for at in range(4):
        for copy in range(out_ref.shape[0]):
            out_ref[copy, pl.ds(at * 8, 8), :] = acc[at]


def synth_kernel(part_ref, keep_ref, fac_ref, out_ref):
    freqs, _, base = out_ref.shape
    block = BLOCK
    total = part_ref[0]
    for source in range(1, part_ref.shape[0]):
        total = total + part_ref[source]
    kept = jnp.where(keep_ref[...] > 0, total, 0.0).astype(BF16).astype(F32)
    kept = kept * math.sqrt(NB / K)
    top = lax.broadcasted_iota(jnp.int32, (2 * CAP, base), 0) < CAP

    def body(i, kept):
        first = pl.multiple_of(i * block, block)
        for j in range(block):
            re = jnp.zeros((2 * CAP, base), F32)
            im = jnp.zeros((2 * CAP, base), F32)
            for pair in range(K // 2):
                fac_re = fac_ref[first + j, pl.ds(pair * 8, 8)].astype(F32)
                fac_im = fac_ref[first + j, pl.ds(16 + pair * 8, 8)].astype(F32)
                kept_re = kept[pair * 8 : pair * 8 + 8, j : j + 1]
                kept_im = kept[16 + pair * 8 : 24 + pair * 8, j : j + 1]
                re = re + (fac_re * kept_re - fac_im * kept_im)
                im = im + (fac_re * kept_im + fac_im * kept_re)
            re = re + pltpu.roll(re, CAP, 0)
            im = im + pltpu.roll(im, CAP, 0)
            out_ref[first + j] = jnp.where(top, re, im).astype(BF16)
        return pltpu.roll(kept, freqs - block, 1)

    lax.fori_loop(0, freqs // block, body, kept)


def final_kernel(target_ref, slots_ref, out_ref):
    rows = lax.broadcasted_iota(jnp.int32, (slots_ref.shape[0], MM), 0)
    for part in range(2):
        placing = jnp.where(rows == target_ref[...] + part * CAP, 1.0, 0.0).astype(BF16)
        out_ref[part] = lax.dot_general(
            slots_ref[...], placing, (((0,), (0,)), ((), ())), preferred_element_type=F32
        ).astype(BF16)


def local(vis_time, owner, counts, factors):
    n_freq = lax.axis_size("freq")
    n_bl = lax.axis_size("bl")
    myself = lax.axis_index("freq")
    base = vis_time.shape[2]
    flat = vis_time.reshape(2 * base, NT)
    owner_row = owner.reshape(1, MM)
    width = 2 * CAP
    hbm = pl.BlockSpec(memory_space=pltpu.HBM)
    wave = jnp.asarray(wave_half())
    outgoing, target = pl.pallas_call(
        dft_kernel,
        in_specs=[hbm, hbm, hbm],
        out_shape=[
            jax.ShapeDtypeStruct((n_freq * width, base), BF16),
            jax.ShapeDtypeStruct((1, MM), jnp.int32),
        ],
        scratch_shapes=[
            pltpu.VMEM((1, MM), jnp.int32),
            pltpu.VMEM((4, 2 * base, CHUNK), BF16),
            pltpu.VMEM((2, CHUNK, 2 * MM), BF16),
            pltpu.SemaphoreType.DMA((7,)),
        ],
        compiler_params=pltpu.CompilerParams(vmem_limit_bytes=40 << 20),
        name="dft",
    )(*(pltpu.with_memory_space_constraint(a, pltpu.HBM) for a in (owner_row, flat, wave)))
    incoming = lax.all_to_all(
        outgoing.reshape(n_freq, width, base), "freq", split_axis=0, concat_axis=0, tiled=True
    )

    slot_rows = myself * width + jnp.arange(CAP, dtype=jnp.int32)
    mine = (target == slot_rows[:, None]).astype(BF16)
    limits = jnp.dot(mine, counts.astype(BF16), preferred_element_type=F32)
    by_freq = jnp.transpose(factors, (1, 2, 3, 0, 4)).reshape(n_freq, 2 * K * CAP, base)

    partial, keep = pl.pallas_call(
        coef_kernel,
        out_shape=[
            jax.ShapeDtypeStruct((n_bl, 2 * K * CAP, n_freq), F32),
            jax.ShapeDtypeStruct((2 * K * CAP, n_freq), F32),
        ],
        compiler_params=pltpu.CompilerParams(vmem_limit_bytes=40 << 20),
        name="coef",
    )(incoming, by_freq, limits)
    partials = lax.all_to_all(partial, "bl", split_axis=0, concat_axis=0, tiled=True)
    synthesis = pl.pallas_call(
        synth_kernel,
        out_shape=jax.ShapeDtypeStruct((n_freq, width, base), BF16),
        compiler_params=pltpu.CompilerParams(vmem_limit_bytes=40 << 20),
        name="synth",
    )(partials, keep, by_freq)
    returned = lax.all_to_all(synthesis, "freq", split_axis=0, concat_axis=0, tiled=True)
    filtered = pl.pallas_call(
        final_kernel,
        out_shape=jax.ShapeDtypeStruct((2, base, MM), BF16),
        compiler_params=pltpu.CompilerParams(vmem_limit_bytes=40 << 20),
        name="final",
    )(target, returned.reshape(n_freq * width, base))
    return filtered[None]


def solution(mesh):
    placed = (P("freq", None, "bl", None), P(), P(), P("freq", None, None, None, "bl"))
    return jax.shard_map(
        local, mesh=mesh, in_specs=placed, out_specs=P("freq", None, "bl", None), check_vma=False
    )
```

```python
import math

import jax
import jax.numpy as jnp
import numpy as np
from jax import lax
from jax.experimental import pallas as pl
from jax.experimental.pallas import tpu as pltpu
from jax.sharding import PartitionSpec as P

NB = 1024
NT = 2048
K = 4
MM = 384
CAP = 4
CHUNK = NT // 4
BLOCK = 32
F32 = jnp.float32
BF16 = jnp.bfloat16


def wave_half():
    phases = np.outer(np.arange(NT // 2), np.arange(MM)) % NT
    angles = phases * (2.0 * math.pi / NT)
    rows = np.concatenate([np.cos(angles), np.sin(angles)], axis=1) / math.sqrt(NT)
    return rows.astype(np.float32).astype(jnp.bfloat16)


def dft_kernel(owner_hbm, vis_hbm, wave_hbm, out_ref, target_ref, owner_ref, vis_ref, wave_ref, sems):
    owners = out_ref.shape[0] // (2 * CAP)
    owner_copy = pltpu.make_async_copy(owner_hbm, owner_ref, sems.at[0])
    owner_copy.start()
    wave_copies, vis_copies = [], {}
    for part in range(2):
        wave_copies.append(
            pltpu.make_async_copy(
                wave_hbm.at[pl.ds(part * CHUNK, CHUNK)], wave_ref.at[part], sems.at[1 + part]
            )
        )
        wave_copies[-1].start()
        for chunk in (part, part + 2):
            vis_copies[chunk] = pltpu.make_async_copy(
                vis_hbm.at[:, pl.ds(chunk * CHUNK, CHUNK)], vis_ref.at[chunk], sems.at[3 + chunk]
            )
            vis_copies[chunk].start()
    owner_copy.wait()
    owner = owner_ref[...]
    hot = owner == lax.broadcasted_iota(jnp.int32, (owners, MM), 0)
    hot = jnp.where(hot, 1.0, 0.0)
    earlier = lax.broadcasted_iota(jnp.int32, (MM, MM), 0) < lax.broadcasted_iota(
        jnp.int32, (MM, MM), 1
    )
    earlier = jnp.where(earlier, 1.0, 0.0).astype(BF16)
    before = jnp.dot(hot.astype(BF16), earlier, preferred_element_type=F32)
    rank = jnp.sum(before * hot, axis=0, keepdims=True).astype(jnp.int32)
    target = owner * (2 * CAP) + rank
    target_ref[...] = target
    target = jnp.concatenate([target, target + CAP], axis=1)
    rows = lax.broadcasted_iota(jnp.int32, (out_ref.shape[0], 2 * MM), 0)
    placing = jnp.where(rows == target, 1.0, 0.0).astype(BF16)

    sign = 1 - 2 * (lax.broadcasted_iota(jnp.int32, (1, 2 * MM), 1) % 2)
    sign = sign.astype(F32)
    spectra = None
    for part in range(2):
        wave_copies[part].wait()
        for half in range(2):
            chunk = part + 2 * half
            vis_copies[chunk].wait()
            product = jnp.dot(vis_ref[chunk], wave_ref[part], preferred_element_type=F32)
            if half == 1:
                product = product * sign
            spectra = product if spectra is None else spectra + product
    base = spectra.shape[0] // 2
    real = spectra[:base, :MM] + spectra[base:, MM:]
    imag = spectra[base:, :MM] - spectra[:base, MM:]
    modes = jnp.concatenate([real, imag], axis=1).astype(BF16)
    out_ref[...] = lax.dot_general(
        placing, modes, (((1,), (1,)), ((), ())), preferred_element_type=F32
    ).astype(BF16)


def coef_kernel(core_ref, vis_ref, own_ref, other_ref, limit_ref, out_ref, keep_ref):
    core = core_ref[0]
    pairs, _, base = vis_ref.shape
    top = lax.broadcasted_iota(jnp.int32, (1, 2 * CAP, base), 1) < CAP
    lanes = lax.broadcasted_iota(jnp.int32, (2 * CAP, pairs), 1)
    ranks = lax.broadcasted_iota(jnp.int32, (2 * K * CAP, pairs), 0) // CAP % K
    limits = jnp.concatenate([limit_ref[...]] * (2 * K), axis=0)
    keep_ref[...] = jnp.where(ranks.astype(F32) < limits, 1.0, 0.0)

    def body(i, acc):
        acc = list(acc)
        for j in range(BLOCK):
            at_freq = i * (BLOCK // 2) + j // 2
            fac_ref, row = (own_ref, 2 * at_freq + core) if j % 2 == 0 else (other_ref, at_freq)
            vis = vis_ref[2 * at_freq + (core if j % 2 == 0 else 1 - core)].astype(F32)
            swapped = pltpu.roll(vis, CAP, 0)
            vis_re = jnp.where(top[0], vis, swapped)
            vis_im = jnp.where(top[0], swapped, vis)
            here = lanes == i * BLOCK + j
            for pair in range(K // 2):
                fac_re = fac_ref[row, pl.ds(pair * 8, 8)].astype(F32)
                fac_im = fac_ref[row, pl.ds(16 + pair * 8, 8)].astype(F32)
                re = jnp.sum(fac_re * vis_re + fac_im * vis_im, axis=1, keepdims=True)
                im = jnp.sum(fac_re * vis_im - fac_im * vis_re, axis=1, keepdims=True)
                acc[pair] = jnp.where(here, re, acc[pair])
                acc[2 + pair] = jnp.where(here, im, acc[2 + pair])
        return tuple(acc)

    zero = jnp.zeros((2 * CAP, pairs), F32)
    acc = lax.fori_loop(0, pairs // BLOCK, body, (zero,) * 4)
    for at in range(4):
        for copy in range(out_ref.shape[0]):
            out_ref[copy, pl.ds(at * 8, 8), :] = acc[at]


def synth_kernel(core_ref, part_ref, keep_ref, own_ref, other_ref, out_ref):
    core = core_ref[0]
    pairs, _, base = out_ref.shape
    total = part_ref[0]
    for source in range(1, part_ref.shape[0]):
        total = total + part_ref[source]
    kept = jnp.where(keep_ref[...] > 0, total, 0.0).astype(BF16).astype(F32)
    kept = kept * math.sqrt(NB / K)
    top = lax.broadcasted_iota(jnp.int32, (2 * CAP, base), 0) < CAP

    def body(i, kept):
        for j in range(BLOCK):
            at_freq = i * (BLOCK // 2) + j // 2
            fac_ref, row = (own_ref, 2 * at_freq + core) if j % 2 == 0 else (other_ref, at_freq)
            re = jnp.zeros((2 * CAP, base), F32)
            im = jnp.zeros((2 * CAP, base), F32)
            for pair in range(K // 2):
                fac_re = fac_ref[row, pl.ds(pair * 8, 8)].astype(F32)
                fac_im = fac_ref[row, pl.ds(16 + pair * 8, 8)].astype(F32)
                kept_re = kept[pair * 8 : pair * 8 + 8, j : j + 1]
                kept_im = kept[16 + pair * 8 : 24 + pair * 8, j : j + 1]
                re = re + (fac_re * kept_re - fac_im * kept_im)
                im = im + (fac_re * kept_im + fac_im * kept_re)
            re = re + pltpu.roll(re, CAP, 0)
            im = im + pltpu.roll(im, CAP, 0)
            filtered = jnp.where(top, re, im).astype(BF16)
            out_ref[2 * at_freq + (core if j % 2 == 0 else 1 - core)] = filtered
        return pltpu.roll(kept, pairs - BLOCK, 1)

    lax.fori_loop(0, pairs // BLOCK, body, kept)


def final_kernel(target_ref, slots_ref, out_ref):
    rows = lax.broadcasted_iota(jnp.int32, (slots_ref.shape[0], MM), 0)
    for part in range(2):
        placing = jnp.where(rows == target_ref[...] + part * CAP, 1.0, 0.0).astype(BF16)
        out_ref[part] = lax.dot_general(
            slots_ref[...], placing, (((0,), (0,)), ((), ())), preferred_element_type=F32
        ).astype(BF16)


def local(vis_time, owner, counts, factors):
    n_freq = lax.axis_size("freq")
    n_bl = lax.axis_size("bl")
    myself = lax.axis_index("freq")
    base = vis_time.shape[2]
    flat = vis_time.reshape(2 * base, NT)
    owner_row = owner.reshape(1, MM)
    width = 2 * CAP
    hbm = pl.BlockSpec(memory_space=pltpu.HBM)
    wave = jnp.asarray(wave_half())
    outgoing, target = pl.pallas_call(
        dft_kernel,
        in_specs=[hbm, hbm, hbm],
        out_shape=[
            jax.ShapeDtypeStruct((n_freq * width, base), BF16),
            jax.ShapeDtypeStruct((1, MM), jnp.int32),
        ],
        scratch_shapes=[
            pltpu.VMEM((1, MM), jnp.int32),
            pltpu.VMEM((4, 2 * base, CHUNK), BF16),
            pltpu.VMEM((2, CHUNK, 2 * MM), BF16),
            pltpu.SemaphoreType.DMA((7,)),
        ],
        compiler_params=pltpu.CompilerParams(vmem_limit_bytes=40 << 20),
        name="dft",
    )(*(pltpu.with_memory_space_constraint(a, pltpu.HBM) for a in (owner_row, flat, wave)))
    n_chip = n_freq // 2
    alike = [[2 * chip + side for chip in range(n_chip)] for side in range(2)]
    swap = [(d, d ^ 1) for d in range(n_freq)]
    chip, core = myself >> 1, myself & 1

    def exchange(rows):
        return lax.all_to_all(
            rows.reshape(n_chip, 2 * width, base),
            "freq",
            split_axis=0,
            concat_axis=0,
            axis_index_groups=alike,
            tiled=True,
        ).reshape(n_freq, width, base)

    incoming = exchange(outgoing)

    factors, _ = lax.optimization_barrier((factors, outgoing))
    by_freq = jnp.transpose(factors, (1, 2, 3, 0, 4)).reshape(n_freq, 2 * K * CAP, base)
    sent = lax.dynamic_slice_in_dim(
        by_freq.reshape(n_chip, 2, 2 * K * CAP, base), 1 - core, 1, 1
    ).reshape(n_chip, 2 * K * CAP, base)
    other = lax.ppermute(sent, "freq", swap)

    side = jnp.arange(2, dtype=jnp.int32)[:, None]
    slot_rows = (2 * chip + (core ^ side)) * width + jnp.arange(CAP, dtype=jnp.int32)
    mine = (target == slot_rows.reshape(2 * CAP, 1)).astype(BF16)
    limits = jnp.dot(mine, counts.astype(BF16), preferred_element_type=F32)
    lane = jnp.arange(n_freq, dtype=jnp.int32)
    chosen = (lane[:, None] == (lane & -2) + core).astype(BF16)
    limits = jnp.dot(limits.astype(BF16), chosen, preferred_element_type=F32)
    limits = jnp.where(lane & 1 == 0, limits[:CAP], limits[CAP:])

    core_word = core.reshape(1)
    smem = pl.BlockSpec(memory_space=pltpu.SMEM)
    vmem = pl.BlockSpec(memory_space=pltpu.VMEM)
    partial, keep = pl.pallas_call(
        coef_kernel,
        in_specs=[smem, vmem, vmem, vmem, vmem],
        out_shape=[
            jax.ShapeDtypeStruct((n_bl, 2 * K * CAP, n_freq), F32),
            jax.ShapeDtypeStruct((2 * K * CAP, n_freq), F32),
        ],
        compiler_params=pltpu.CompilerParams(vmem_limit_bytes=40 << 20),
        name="coef",
    )(core_word, incoming, by_freq, other, limits)
    partials = lax.all_to_all(partial, "bl", split_axis=0, concat_axis=0, tiled=True)
    synthesis = pl.pallas_call(
        synth_kernel,
        in_specs=[smem, vmem, vmem, vmem, vmem],
        out_shape=jax.ShapeDtypeStruct((n_freq, width, base), BF16),
        compiler_params=pltpu.CompilerParams(vmem_limit_bytes=40 << 20),
        name="synth",
    )(core_word, partials, keep, by_freq, other)
    returned = exchange(synthesis)
    filtered = pl.pallas_call(
        final_kernel,
        out_shape=jax.ShapeDtypeStruct((2, base, MM), BF16),
        compiler_params=pltpu.CompilerParams(vmem_limit_bytes=40 << 20),
        name="final",
    )(target, returned.reshape(n_freq * width, base))
    return filtered[None]


def solution(mesh):
    placed = (P("freq", None, "bl", None), P(), P(), P("freq", None, None, None, "bl"))
    return jax.shard_map(
        local, mesh=mesh, in_specs=placed, out_specs=P("freq", None, "bl", None), check_vma=False
    )
```

```python
import math

import jax
import jax.numpy as jnp
import numpy as np
from jax import lax
from jax.experimental import pallas as pl
from jax.experimental.pallas import tpu as pltpu
from jax.sharding import PartitionSpec as P

NB = 1024
NT = 2048
K = 4
MM = 384
CAP = 4
CHUNK = NT // 4
BLOCK = 32
F32 = jnp.float32
BF16 = jnp.bfloat16


def wave_half():
    phases = np.outer(np.arange(NT // 2), np.arange(MM)) % NT
    angles = phases * (2.0 * math.pi / NT)
    rows = np.concatenate([np.cos(angles), np.sin(angles)], axis=1) / math.sqrt(NT)
    return rows.astype(np.float32).astype(jnp.bfloat16)


def dft_kernel(owner_hbm, vis_hbm, wave_hbm, out_ref, target_ref, owner_ref, vis_ref, wave_ref, sems):
    owners = out_ref.shape[0] // (2 * CAP)
    owner_copy = pltpu.make_async_copy(owner_hbm, owner_ref, sems.at[0])
    owner_copy.start()
    wave_copies, vis_copies = [], {}
    for part in range(2):
        wave_copies.append(
            pltpu.make_async_copy(
                wave_hbm.at[pl.ds(part * CHUNK, CHUNK)], wave_ref.at[part], sems.at[1 + part]
            )
        )
        wave_copies[-1].start()
        for chunk in (part, part + 2):
            vis_copies[chunk] = pltpu.make_async_copy(
                vis_hbm.at[:, pl.ds(chunk * CHUNK, CHUNK)], vis_ref.at[chunk], sems.at[3 + chunk]
            )
            vis_copies[chunk].start()
    owner_copy.wait()
    owner = owner_ref[...]
    hot = owner == lax.broadcasted_iota(jnp.int32, (owners, MM), 0)
    hot = jnp.where(hot, 1.0, 0.0)
    earlier = lax.broadcasted_iota(jnp.int32, (MM, MM), 0) < lax.broadcasted_iota(
        jnp.int32, (MM, MM), 1
    )
    earlier = jnp.where(earlier, 1.0, 0.0).astype(BF16)
    before = jnp.dot(hot.astype(BF16), earlier, preferred_element_type=F32)
    rank = jnp.sum(before * hot, axis=0, keepdims=True).astype(jnp.int32)
    target = owner * (2 * CAP) + rank
    target_ref[...] = target
    target = jnp.concatenate([target, target + CAP], axis=1)
    rows = lax.broadcasted_iota(jnp.int32, (out_ref.shape[0], 2 * MM), 0)
    placing = jnp.where(rows == target, 1.0, 0.0).astype(BF16)

    sign = 1 - 2 * (lax.broadcasted_iota(jnp.int32, (1, 2 * MM), 1) % 2)
    sign = sign.astype(F32)
    spectra = None
    for part in range(2):
        wave_copies[part].wait()
        for half in range(2):
            chunk = part + 2 * half
            vis_copies[chunk].wait()
            product = jnp.dot(vis_ref[chunk], wave_ref[part], preferred_element_type=F32)
            if half == 1:
                product = product * sign
            spectra = product if spectra is None else spectra + product
    base = spectra.shape[0] // 2
    real = spectra[:base, :MM] + spectra[base:, MM:]
    imag = spectra[base:, :MM] - spectra[:base, MM:]
    modes = jnp.concatenate([real, imag], axis=1).astype(BF16)
    out_ref[...] = lax.dot_general(
        placing, modes, (((1,), (1,)), ((), ())), preferred_element_type=F32
    ).astype(BF16)


def relay_kernel(core_ref, fac_ref, own_ref, sent_ref, rows_ref):
    core = core_ref[0]

    def body(i, carry):
        for out_ref, side in ((own_ref, core), (sent_ref, 1 - core)):
            for lane in range(rows_ref.shape[0]):
                for part in range(2):
                    for slot in range(CAP):
                        rows = fac_ref[slot, 2 * i + side, part, :, pl.ds(lane * 128, 128)]
                        first = part * K * CAP + slot
                        rows_ref[lane, pl.ds(first, K, stride=CAP), :] = rows.astype(F32)
                out_ref[i, :, pl.ds(lane * 128, 128)] = rows_ref[lane].astype(BF16)
        return carry

    lax.fori_loop(0, own_ref.shape[0], body, 0, unroll=4)


def coef_kernel(core_ref, vis_ref, own_ref, other_ref, limit_ref, out_ref, keep_ref):
    core = core_ref[0]
    pairs, _, base = vis_ref.shape
    top = lax.broadcasted_iota(jnp.int32, (1, 2 * CAP, base), 1) < CAP
    lanes = lax.broadcasted_iota(jnp.int32, (2 * CAP, pairs), 1)
    ranks = lax.broadcasted_iota(jnp.int32, (2 * K * CAP, pairs), 0) // CAP % K
    limits = jnp.concatenate([limit_ref[...]] * (2 * K), axis=0)
    keep_ref[...] = jnp.where(ranks.astype(F32) < limits, 1.0, 0.0)

    def body(i, acc):
        acc = list(acc)
        for j in range(BLOCK):
            at_freq = i * (BLOCK // 2) + j // 2
            fac_ref = own_ref if j % 2 == 0 else other_ref
            vis = vis_ref[2 * at_freq + (core if j % 2 == 0 else 1 - core)].astype(F32)
            swapped = pltpu.roll(vis, CAP, 0)
            vis_re = jnp.where(top[0], vis, swapped)
            vis_im = jnp.where(top[0], swapped, vis)
            here = lanes == i * BLOCK + j
            for pair in range(K // 2):
                fac_re = fac_ref[at_freq, pl.ds(pair * 8, 8)].astype(F32)
                fac_im = fac_ref[at_freq, pl.ds(16 + pair * 8, 8)].astype(F32)
                re = jnp.sum(fac_re * vis_re + fac_im * vis_im, axis=1, keepdims=True)
                im = jnp.sum(fac_re * vis_im - fac_im * vis_re, axis=1, keepdims=True)
                acc[pair] = jnp.where(here, re, acc[pair])
                acc[2 + pair] = jnp.where(here, im, acc[2 + pair])
        return tuple(acc)

    zero = jnp.zeros((2 * CAP, pairs), F32)
    acc = lax.fori_loop(0, pairs // BLOCK, body, (zero,) * 4)
    for at in range(4):
        for copy in range(out_ref.shape[0]):
            out_ref[copy, pl.ds(at * 8, 8), :] = acc[at]


def synth_kernel(core_ref, part_ref, keep_ref, own_ref, other_ref, out_ref):
    core = core_ref[0]
    pairs, _, base = out_ref.shape
    total = part_ref[0]
    for source in range(1, part_ref.shape[0]):
        total = total + part_ref[source]
    kept = jnp.where(keep_ref[...] > 0, total, 0.0).astype(BF16).astype(F32)
    kept = kept * math.sqrt(NB / K)
    top = lax.broadcasted_iota(jnp.int32, (2 * CAP, base), 0) < CAP

    def body(i, kept):
        for j in range(BLOCK):
            at_freq = i * (BLOCK // 2) + j // 2
            fac_ref = own_ref if j % 2 == 0 else other_ref
            re = jnp.zeros((2 * CAP, base), F32)
            im = jnp.zeros((2 * CAP, base), F32)
            for pair in range(K // 2):
                fac_re = fac_ref[at_freq, pl.ds(pair * 8, 8)].astype(F32)
                fac_im = fac_ref[at_freq, pl.ds(16 + pair * 8, 8)].astype(F32)
                kept_re = kept[pair * 8 : pair * 8 + 8, j : j + 1]
                kept_im = kept[16 + pair * 8 : 24 + pair * 8, j : j + 1]
                re = re + (fac_re * kept_re - fac_im * kept_im)
                im = im + (fac_re * kept_im + fac_im * kept_re)
            re = re + pltpu.roll(re, CAP, 0)
            im = im + pltpu.roll(im, CAP, 0)
            filtered = jnp.where(top, re, im).astype(BF16)
            out_ref[2 * at_freq + (core if j % 2 == 0 else 1 - core)] = filtered
        return pltpu.roll(kept, pairs - BLOCK, 1)

    lax.fori_loop(0, pairs // BLOCK, body, kept)


def final_kernel(target_ref, slots_ref, out_hbm, out_ref, sems):
    rows = lax.broadcasted_iota(jnp.int32, (slots_ref.shape[0], MM), 0)
    copies = []
    for part in range(2):
        placing = jnp.where(rows == target_ref[...] + part * CAP, 1.0, 0.0).astype(BF16)
        out_ref[part] = lax.dot_general(
            slots_ref[...], placing, (((0,), (0,)), ((), ())), preferred_element_type=F32
        ).astype(BF16)
        copies.append(pltpu.make_async_copy(out_ref.at[part], out_hbm.at[part], sems.at[part]))
        copies[part].start()
    for copy in copies:
        copy.wait()


def local(vis_time, owner, counts, factors):
    n_chip = lax.axis_size("chip")
    n_freq = n_chip * lax.axis_size("core")
    n_bl = lax.axis_size("bl")
    chip, core = lax.axis_index("chip"), lax.axis_index("core")
    base = vis_time.shape[2]
    flat = vis_time.reshape(2 * base, NT)
    owner_row = owner.reshape(1, MM)
    width = 2 * CAP
    hbm = pl.BlockSpec(memory_space=pltpu.HBM)
    wave = jnp.asarray(wave_half())
    outgoing, target = pl.pallas_call(
        dft_kernel,
        in_specs=[hbm, hbm, hbm],
        out_shape=[
            jax.ShapeDtypeStruct((n_freq * width, base), BF16),
            jax.ShapeDtypeStruct((1, MM), jnp.int32),
        ],
        scratch_shapes=[
            pltpu.VMEM((1, MM), jnp.int32),
            pltpu.VMEM((4, 2 * base, CHUNK), BF16),
            pltpu.VMEM((2, CHUNK, 2 * MM), BF16),
            pltpu.SemaphoreType.DMA((7,)),
        ],
        compiler_params=pltpu.CompilerParams(vmem_limit_bytes=24 << 20),
        name="dft",
    )(*(pltpu.with_memory_space_constraint(a, pltpu.HBM) for a in (owner_row, flat, wave)))
    def exchange(rows):
        return lax.all_to_all(
            rows.reshape(n_chip, 2 * width, base), "chip", split_axis=0, concat_axis=0, tiled=True
        ).reshape(n_freq, width, base)

    incoming = exchange(outgoing)

    factors, _ = lax.optimization_barrier((factors, outgoing))
    core_word = core.reshape(1)
    smem = pl.BlockSpec(memory_space=pltpu.SMEM)
    vmem = pl.BlockSpec(memory_space=pltpu.VMEM)
    own, sent = pl.pallas_call(
        relay_kernel,
        grid=(4,),
        in_specs=[smem, pl.BlockSpec((CAP, n_freq // 4, 2, K, base), lambda i: (0, i, 0, 0, 0))],
        out_specs=[pl.BlockSpec((n_chip // 4, 2 * K * CAP, base), lambda i: (i, 0, 0))] * 2,
        out_shape=[jax.ShapeDtypeStruct((n_chip, 2 * K * CAP, base), BF16)] * 2,
        scratch_shapes=[pltpu.VMEM((base // 128, 2 * K * CAP, 128), F32)],
        compiler_params=pltpu.CompilerParams(vmem_limit_bytes=8 << 20),
        name="relay",
    )(core_word, pltpu.with_memory_space_constraint(factors, pltpu.HBM))
    other = lax.ppermute(sent, "core", [(0, 1), (1, 0)])

    side = jnp.arange(2, dtype=jnp.int32)[:, None]
    slot_rows = (2 * chip + (core ^ side)) * width + jnp.arange(CAP, dtype=jnp.int32)
    mine = (target == slot_rows.reshape(2 * CAP, 1)).astype(BF16)
    limits = jnp.dot(mine, counts.astype(BF16), preferred_element_type=F32)
    lane = jnp.arange(n_freq, dtype=jnp.int32)
    chosen = (lane[:, None] == (lane & -2) + core).astype(BF16)
    limits = jnp.dot(limits.astype(BF16), chosen, preferred_element_type=F32)
    limits = jnp.where(lane & 1 == 0, limits[:CAP], limits[CAP:])

    partial, keep = pl.pallas_call(
        coef_kernel,
        in_specs=[smem, vmem, vmem, vmem, vmem],
        out_shape=[
            jax.ShapeDtypeStruct((n_bl, 2 * K * CAP, n_freq), F32),
            jax.ShapeDtypeStruct((2 * K * CAP, n_freq), F32),
        ],
        compiler_params=pltpu.CompilerParams(vmem_limit_bytes=8 << 20),
        name="coef",
    )(core_word, incoming, own, other, limits)
    partials = lax.all_to_all(partial, "bl", split_axis=0, concat_axis=0, tiled=True)
    synthesis = pl.pallas_call(
        synth_kernel,
        in_specs=[smem, vmem, vmem, vmem, vmem],
        out_shape=jax.ShapeDtypeStruct((n_freq, width, base), BF16),
        compiler_params=pltpu.CompilerParams(vmem_limit_bytes=8 << 20),
        name="synth",
    )(core_word, partials, keep, own, other)
    returned = exchange(synthesis)
    filtered = pl.pallas_call(
        final_kernel,
        out_specs=hbm,
        out_shape=jax.ShapeDtypeStruct((2, base, MM), BF16),
        scratch_shapes=[pltpu.VMEM((2, base, MM), BF16), pltpu.SemaphoreType.DMA((2,))],
        compiler_params=pltpu.CompilerParams(vmem_limit_bytes=16 << 20),
        name="final",
    )(target, returned.reshape(n_freq * width, base))
    return filtered[None]


def solution(mesh):
    n_freq, n_bl = mesh.devices.shape
    by_chip = jax.sharding.Mesh(
        mesh.devices.reshape(n_freq // 2, 2, n_bl), ("chip", "core", "bl")
    )
    freq = ("chip", "core")
    placed = (P(freq, None, "bl", None), P(), P(), P(freq, None, None, None, "bl"))
    return jax.shard_map(
        local, mesh=by_chip, in_specs=placed, out_specs=P(freq, None, "bl", None), check_vma=False
    )
```

```python
import math

import jax
import jax.numpy as jnp
import numpy as np
from jax import lax
from jax.experimental import pallas as pl
from jax.experimental.pallas import tpu as pltpu
from jax.sharding import PartitionSpec as P

NB = 1024
NT = 2048
K = 4
MM = 384
CAP = 4
CHUNK = NT // 4
BLOCK = 32
F32 = jnp.float32
BF16 = jnp.bfloat16


def wave_half():
    phases = np.outer(np.arange(NT // 2), np.arange(MM)) % NT
    angles = phases * (2.0 * math.pi / NT)
    rows = np.concatenate([np.cos(angles), np.sin(angles)], axis=1) / math.sqrt(NT)
    return rows.astype(np.float32).astype(jnp.bfloat16)


def dft_kernel(
    owner_hbm, vis_hbm, wave_hbm, out_hbm, target_ref, owner_ref, vis_ref, wave_ref, out_ref, sems
):
    chips, _, width, base = out_ref.shape
    owners = chips * width // CAP
    owner_copy = pltpu.make_async_copy(owner_hbm, owner_ref, sems.at[0])
    owner_copy.start()
    wave_copies, vis_copies = [], {}
    for part in range(2):
        wave_copies.append(
            pltpu.make_async_copy(
                wave_hbm.at[pl.ds(part * CHUNK, CHUNK)], wave_ref.at[part], sems.at[1 + part]
            )
        )
        wave_copies[-1].start()
        for chunk in (part, part + 2):
            vis_copies[chunk] = pltpu.make_async_copy(
                vis_hbm.at[:, pl.ds(chunk * CHUNK, CHUNK)], vis_ref.at[chunk], sems.at[3 + chunk]
            )
            vis_copies[chunk].start()
    owner_copy.wait()
    owner = owner_ref[...]
    hot = owner == lax.broadcasted_iota(jnp.int32, (owners, MM), 0)
    hot = jnp.where(hot, 1.0, 0.0)
    earlier = lax.broadcasted_iota(jnp.int32, (MM, MM), 0) < lax.broadcasted_iota(
        jnp.int32, (MM, MM), 1
    )
    earlier = jnp.where(earlier, 1.0, 0.0).astype(BF16)
    before = jnp.dot(hot.astype(BF16), earlier, preferred_element_type=F32)
    rank = jnp.sum(before * hot, axis=0, keepdims=True).astype(jnp.int32)
    target = owner * CAP + rank
    target_ref[...] = target
    rows = lax.broadcasted_iota(jnp.int32, (owners * CAP, MM), 0)
    placing = jnp.where(rows == target, 1.0, 0.0).astype(BF16)

    sign = 1 - 2 * (lax.broadcasted_iota(jnp.int32, (1, 2 * MM), 1) % 2)
    sign = sign.astype(F32)
    spectra = None
    for part in range(2):
        wave_copies[part].wait()
        for half in range(2):
            chunk = part + 2 * half
            vis_copies[chunk].wait()
            product = jnp.dot(vis_ref[chunk], wave_ref[part], preferred_element_type=F32)
            if half == 1:
                product = product * sign
            spectra = product if spectra is None else spectra + product
    real = spectra[:base, :MM] + spectra[base:, MM:]
    imag = spectra[base:, :MM] - spectra[:base, MM:]
    out_copies = []
    for part, modes in enumerate((real, imag)):
        placed = lax.dot_general(
            placing, modes.astype(BF16), (((1,), (1,)), ((), ())), preferred_element_type=F32
        )
        out_ref[:, part] = placed.astype(BF16).reshape(chips, width, base)
        out_copies.append(
            pltpu.make_async_copy(out_ref.at[:, part], out_hbm.at[:, part], sems.at[7 + part])
        )
        out_copies[part].start()
    for copy in out_copies:
        copy.wait()


def relay_kernel(core_ref, fac_ref, own_ref, sent_ref, rows_ref):
    core = core_ref[0]

    def body(i, carry):
        for out_ref, side in ((own_ref, core), (sent_ref, 1 - core)):
            for lane in range(rows_ref.shape[0]):
                for part in range(2):
                    for slot in range(CAP):
                        rows = fac_ref[slot, 2 * i + side, part, :, pl.ds(lane * 128, 128)]
                        first = part * K * CAP + slot
                        rows_ref[lane, pl.ds(first, K, stride=CAP), :] = rows.astype(F32)
                out_ref[i, :, pl.ds(lane * 128, 128)] = rows_ref[lane].astype(BF16)
        return carry

    lax.fori_loop(0, own_ref.shape[0], body, 0, unroll=4)


def coef_kernel(core_ref, vis_ref, own_ref, other_ref, limit_ref, out_ref, keep_ref):
    core = core_ref[0]
    chips, _, width, base = vis_ref.shape
    pairs = 2 * chips
    mine = lax.broadcasted_iota(jnp.int32, (width, base), 0) // CAP == core
    lanes = lax.broadcasted_iota(jnp.int32, (width, pairs), 1)
    ranks = lax.broadcasted_iota(jnp.int32, (2 * K * CAP, pairs), 0) // CAP % K
    limits = jnp.concatenate([limit_ref[...]] * (2 * K), axis=0)
    keep_ref[...] = jnp.where(ranks.astype(F32) < limits, 1.0, 0.0)

    def body(i, acc):
        acc = list(acc)
        for j in range(BLOCK // 2):
            freq = i * (BLOCK // 2) + j
            vis = [vis_ref[freq, part].astype(F32) for part in range(2)]
            swapped = [pltpu.roll(v, CAP, 0) for v in vis]
            for side, fac_ref in enumerate((own_ref, other_ref)):
                first, second = (vis, swapped) if side == 0 else (swapped, vis)
                vis_re = jnp.where(mine, first[0], second[0])
                vis_im = jnp.where(mine, first[1], second[1])
                here = lanes == 2 * freq + side
                for pair in range(K // 2):
                    fac_re = fac_ref[freq, pl.ds(pair * 8, 8)].astype(F32)
                    fac_im = fac_ref[freq, pl.ds(16 + pair * 8, 8)].astype(F32)
                    re = jnp.sum(fac_re * vis_re + fac_im * vis_im, axis=1, keepdims=True)
                    im = jnp.sum(fac_re * vis_im - fac_im * vis_re, axis=1, keepdims=True)
                    acc[pair] = jnp.where(here, re, acc[pair])
                    acc[2 + pair] = jnp.where(here, im, acc[2 + pair])
        return tuple(acc)

    zero = jnp.zeros((width, pairs), F32)
    acc = lax.fori_loop(0, pairs // BLOCK, body, (zero,) * 4)
    for at in range(4):
        for copy in range(out_ref.shape[0]):
            out_ref[copy, pl.ds(at * 8, 8), :] = acc[at]


def synth_kernel(core_ref, part_ref, keep_ref, own_ref, other_ref, out_ref):
    core = core_ref[0]
    chips, _, width, base = out_ref.shape
    pairs = 2 * chips
    total = part_ref[0]
    for source in range(1, part_ref.shape[0]):
        total = total + part_ref[source]
    kept = jnp.where(keep_ref[...] > 0, total, 0.0).astype(BF16).astype(F32)
    kept = kept * math.sqrt(NB / K)
    mine = lax.broadcasted_iota(jnp.int32, (width, base), 0) // CAP == core

    def body(i, kept):
        for j in range(BLOCK // 2):
            freq = i * (BLOCK // 2) + j
            sums = []
            for side, fac_ref in enumerate((own_ref, other_ref)):
                re = jnp.zeros((width, base), F32)
                im = jnp.zeros((width, base), F32)
                lane = 2 * j + side
                for pair in range(K // 2):
                    fac_re = fac_ref[freq, pl.ds(pair * 8, 8)].astype(F32)
                    fac_im = fac_ref[freq, pl.ds(16 + pair * 8, 8)].astype(F32)
                    kept_re = kept[pair * 8 : pair * 8 + 8, lane : lane + 1]
                    kept_im = kept[16 + pair * 8 : 24 + pair * 8, lane : lane + 1]
                    re = re + (fac_re * kept_re - fac_im * kept_im)
                    im = im + (fac_re * kept_im + fac_im * kept_re)
                sums.append((re + pltpu.roll(re, CAP, 0), im + pltpu.roll(im, CAP, 0)))
            for part in range(2):
                out_ref[freq, part] = jnp.where(mine, sums[0][part], sums[1][part]).astype(BF16)
        return pltpu.roll(kept, pairs - BLOCK, 1)

    lax.fori_loop(0, pairs // BLOCK, body, kept)


def final_kernel(target_ref, slots_ref, out_hbm, out_ref, sems):
    chips, _, width, base = slots_ref.shape
    rows = lax.broadcasted_iota(jnp.int32, (chips * width, MM), 0)
    placing = jnp.where(rows == target_ref[...], 1.0, 0.0).astype(BF16)
    copies = []
    for part in range(2):
        slots = slots_ref[:, part].reshape(chips * width, base)
        out_ref[part] = lax.dot_general(
            slots, placing, (((0,), (0,)), ((), ())), preferred_element_type=F32
        ).astype(BF16)
        copies.append(pltpu.make_async_copy(out_ref.at[part], out_hbm.at[part], sems.at[part]))
        copies[part].start()
    for copy in copies:
        copy.wait()


def local(vis_time, owner, counts, factors):
    n_chip = lax.axis_size("chip")
    n_freq = n_chip * lax.axis_size("core")
    n_bl = lax.axis_size("bl")
    chip, core = lax.axis_index("chip"), lax.axis_index("core")
    base = vis_time.shape[2]
    flat = vis_time.reshape(2 * base, NT)
    owner_row = owner.reshape(1, MM)
    width = 2 * CAP
    hbm = pl.BlockSpec(memory_space=pltpu.HBM)
    vmem = pl.BlockSpec(memory_space=pltpu.VMEM)
    smem = pl.BlockSpec(memory_space=pltpu.SMEM)
    wave = jnp.asarray(wave_half())
    outgoing, target = pl.pallas_call(
        dft_kernel,
        in_specs=[hbm, hbm, hbm],
        out_specs=[hbm, vmem],
        out_shape=[
            jax.ShapeDtypeStruct((n_chip, 2, width, base), BF16),
            jax.ShapeDtypeStruct((1, MM), jnp.int32),
        ],
        scratch_shapes=[
            pltpu.VMEM((1, MM), jnp.int32),
            pltpu.VMEM((4, 2 * base, CHUNK), BF16),
            pltpu.VMEM((2, CHUNK, 2 * MM), BF16),
            pltpu.VMEM((n_chip, 2, width, base), BF16),
            pltpu.SemaphoreType.DMA((9,)),
        ],
        compiler_params=pltpu.CompilerParams(vmem_limit_bytes=24 << 20),
        name="dft",
    )(*(pltpu.with_memory_space_constraint(a, pltpu.HBM) for a in (owner_row, flat, wave)))
    def exchange(rows):
        return lax.all_to_all(rows, "chip", split_axis=0, concat_axis=0, tiled=True)

    incoming = exchange(outgoing)

    factors, _ = lax.optimization_barrier((factors, outgoing))
    core_word = core.reshape(1)
    own, sent = pl.pallas_call(
        relay_kernel,
        grid=(4,),
        in_specs=[smem, pl.BlockSpec((CAP, n_freq // 4, 2, K, base), lambda i: (0, i, 0, 0, 0))],
        out_specs=[pl.BlockSpec((n_chip // 4, 2 * K * CAP, base), lambda i: (i, 0, 0))] * 2,
        out_shape=[jax.ShapeDtypeStruct((n_chip, 2 * K * CAP, base), BF16)] * 2,
        scratch_shapes=[pltpu.VMEM((base // 128, 2 * K * CAP, 128), F32)],
        compiler_params=pltpu.CompilerParams(vmem_limit_bytes=8 << 20),
        name="relay",
    )(core_word, pltpu.with_memory_space_constraint(factors, pltpu.HBM))
    other = lax.ppermute(sent, "core", [(0, 1), (1, 0)])

    side = jnp.arange(2, dtype=jnp.int32)[:, None]
    slot_rows = (2 * chip + (core ^ side)) * CAP + jnp.arange(CAP, dtype=jnp.int32)
    mine = (target == slot_rows.reshape(2 * CAP, 1)).astype(BF16)
    limits = jnp.dot(mine, counts.astype(BF16), preferred_element_type=F32)
    lane = jnp.arange(n_freq, dtype=jnp.int32)
    chosen = (lane[:, None] == (lane & -2) + core).astype(BF16)
    limits = jnp.dot(limits.astype(BF16), chosen, preferred_element_type=F32)
    limits = jnp.where(lane & 1 == 0, limits[:CAP], limits[CAP:])

    partial, keep = pl.pallas_call(
        coef_kernel,
        in_specs=[smem, vmem, vmem, vmem, vmem],
        out_shape=[
            jax.ShapeDtypeStruct((n_bl, 2 * K * CAP, n_freq), F32),
            jax.ShapeDtypeStruct((2 * K * CAP, n_freq), F32),
        ],
        compiler_params=pltpu.CompilerParams(vmem_limit_bytes=8 << 20),
        name="coef",
    )(core_word, incoming, own, other, limits)
    partials = lax.all_to_all(partial, "bl", split_axis=0, concat_axis=0, tiled=True)
    synthesis = pl.pallas_call(
        synth_kernel,
        in_specs=[smem, vmem, vmem, vmem, vmem],
        out_shape=jax.ShapeDtypeStruct((n_chip, 2, width, base), BF16),
        compiler_params=pltpu.CompilerParams(vmem_limit_bytes=8 << 20),
        name="synth",
    )(core_word, partials, keep, own, other)
    returned = exchange(synthesis)
    filtered = pl.pallas_call(
        final_kernel,
        out_specs=hbm,
        out_shape=jax.ShapeDtypeStruct((2, base, MM), BF16),
        scratch_shapes=[pltpu.VMEM((2, base, MM), BF16), pltpu.SemaphoreType.DMA((2,))],
        compiler_params=pltpu.CompilerParams(vmem_limit_bytes=16 << 20),
        name="final",
    )(target, returned)
    return filtered[None]


def solution(mesh):
    n_freq, n_bl = mesh.devices.shape
    by_chip = jax.sharding.Mesh(
        mesh.devices.reshape(n_freq // 2, 2, n_bl), ("chip", "core", "bl")
    )
    freq = ("chip", "core")
    placed = (P(freq, None, "bl", None), P(), P(), P(freq, None, None, None, "bl"))
    return jax.shard_map(
        local, mesh=by_chip, in_specs=placed, out_specs=P(freq, None, "bl", None), check_vma=False
    )
```

```python
import math

import jax
import jax.numpy as jnp
import numpy as np
from jax import lax
from jax.experimental import pallas as pl
from jax.experimental.pallas import tpu as pltpu
from jax.sharding import PartitionSpec as P

NB = 1024
NT = 2048
K = 4
MM = 384
CAP = 4
CHUNK = NT // 4
BLOCK = 64
F32 = jnp.float32
BF16 = jnp.bfloat16


def wave_half():
    phases = np.outer(np.arange(NT // 2), np.arange(MM)) % NT
    angles = phases * (2.0 * math.pi / NT)
    rows = np.concatenate([np.cos(angles), np.sin(angles)], axis=1) / math.sqrt(NT)
    return rows.astype(np.float32).astype(jnp.bfloat16)


def dft_kernel(
    owner_hbm, vis_hbm, wave_hbm, out_hbm, target_ref, owner_ref, vis_ref, wave_ref, out_ref, sems
):
    chips, _, width, base = out_ref.shape
    owners = chips * width // CAP
    owner_copy = pltpu.make_async_copy(owner_hbm, owner_ref, sems.at[0])
    owner_copy.start()
    wave_copies, vis_copies = [], {}
    for part in range(2):
        wave_copies.append(
            pltpu.make_async_copy(
                wave_hbm.at[pl.ds(part * CHUNK, CHUNK)], wave_ref.at[part], sems.at[1 + part]
            )
        )
        wave_copies[-1].start()
        for chunk in (part, part + 2):
            vis_copies[chunk] = pltpu.make_async_copy(
                vis_hbm.at[:, pl.ds(chunk * CHUNK, CHUNK)], vis_ref.at[chunk], sems.at[3 + chunk]
            )
            vis_copies[chunk].start()
    owner_copy.wait()
    owner = owner_ref[...]
    hot = owner == lax.broadcasted_iota(jnp.int32, (owners, MM), 0)
    hot = jnp.where(hot, 1.0, 0.0)
    earlier = lax.broadcasted_iota(jnp.int32, (MM, MM), 0) < lax.broadcasted_iota(
        jnp.int32, (MM, MM), 1
    )
    earlier = jnp.where(earlier, 1.0, 0.0).astype(BF16)
    before = jnp.dot(hot.astype(BF16), earlier, preferred_element_type=F32)
    rank = jnp.sum(before * hot, axis=0, keepdims=True).astype(jnp.int32)
    target = owner * CAP + rank
    target_ref[...] = target
    rows = lax.broadcasted_iota(jnp.int32, (owners * CAP, MM), 0)
    placing = jnp.where(rows == target, 1.0, 0.0).astype(BF16)

    sign = 1 - 2 * (lax.broadcasted_iota(jnp.int32, (1, 2 * MM), 1) % 2)
    sign = sign.astype(F32)
    spectra = None
    for part in range(2):
        wave_copies[part].wait()
        for half in range(2):
            chunk = part + 2 * half
            vis_copies[chunk].wait()
            product = jnp.dot(vis_ref[chunk], wave_ref[part], preferred_element_type=F32)
            if half == 1:
                product = product * sign
            spectra = product if spectra is None else spectra + product
    real = spectra[:base, :MM] + spectra[base:, MM:]
    imag = spectra[base:, :MM] - spectra[:base, MM:]
    out_copies = []
    for part, modes in enumerate((real, imag)):
        placed = lax.dot_general(
            placing, modes.astype(BF16), (((1,), (1,)), ((), ())), preferred_element_type=F32
        )
        out_ref[:, part] = placed.astype(BF16).reshape(chips, width, base)
        out_copies.append(
            pltpu.make_async_copy(out_ref.at[:, part], out_hbm.at[:, part], sems.at[7 + part])
        )
        out_copies[part].start()
    for copy in out_copies:
        copy.wait()


def relay_kernel(core_ref, fac_ref, own_ref, sent_ref, rows_ref):
    core = core_ref[0]

    def body(i, carry):
        for out_ref, side in ((own_ref, core), (sent_ref, 1 - core)):
            for lane in range(rows_ref.shape[0]):
                for part in range(2):
                    for slot in range(CAP):
                        rows = fac_ref[slot, 2 * i + side, part, :, pl.ds(lane * 128, 128)]
                        first = part * K * CAP + slot
                        rows_ref[lane, pl.ds(first, K, stride=CAP), :] = rows.astype(F32)
                out_ref[i, :, pl.ds(lane * 128, 128)] = rows_ref[lane, : out_ref.shape[1]].astype(BF16)
        return carry

    lax.fori_loop(0, own_ref.shape[0], body, 0, unroll=4)


def coef_kernel(core_ref, vis_ref, own_ref, other_ref, limit_ref, out_ref, keep_ref):
    core = core_ref[0]
    chips, _, width, base = vis_ref.shape
    pairs = 2 * chips
    mine = lax.broadcasted_iota(jnp.int32, (width, base), 0) // CAP == core
    lanes = lax.broadcasted_iota(jnp.int32, (width, pairs), 1)
    ranks = lax.broadcasted_iota(jnp.int32, (2 * K * CAP, pairs), 0) // CAP % K
    limits = jnp.concatenate([limit_ref[...]] * (2 * K), axis=0)
    keep_ref[...] = jnp.where(ranks.astype(F32) < limits, 1.0, 0.0)

    def body(i, acc):
        acc = list(acc)
        for j in range(BLOCK // 2):
            freq = i * (BLOCK // 2) + j
            vis = [vis_ref[freq, part].astype(F32) for part in range(2)]
            swapped = [pltpu.roll(v, CAP, 0) for v in vis]
            for side, fac_ref in enumerate((own_ref, other_ref)):
                first, second = (vis, swapped) if side == 0 else (swapped, vis)
                vis_re = jnp.where(mine, first[0], second[0])
                vis_im = jnp.where(mine, first[1], second[1])
                here = lanes == 2 * freq + side
                for pair in range(K // 2):
                    fac_re = fac_ref[freq, pl.ds(pair * 8, 8)].astype(F32)
                    fac_im = fac_ref[freq, pl.ds(16 + pair * 8, 8)].astype(F32)
                    re = jnp.sum(fac_re * vis_re + fac_im * vis_im, axis=1, keepdims=True)
                    im = jnp.sum(fac_re * vis_im - fac_im * vis_re, axis=1, keepdims=True)
                    acc[pair] = jnp.where(here, re, acc[pair])
                    acc[2 + pair] = jnp.where(here, im, acc[2 + pair])
        return tuple(acc)

    zero = jnp.zeros((width, pairs), F32)
    acc = lax.fori_loop(0, pairs // BLOCK, body, (zero,) * 4)
    for at in range(4):
        for copy in range(out_ref.shape[0]):
            out_ref[copy, pl.ds(at * 8, 8), :] = acc[at]


def synth_kernel(core_ref, part_ref, keep_ref, own_ref, other_ref, out_ref):
    core = core_ref[0]
    chips, _, width, base = out_ref.shape
    pairs = 2 * chips
    total = part_ref[0]
    for source in range(1, part_ref.shape[0]):
        total = total + part_ref[source]
    kept = jnp.where(keep_ref[...] > 0, total, 0.0).astype(BF16).astype(F32)
    kept = kept * math.sqrt(NB / K)
    mine = lax.broadcasted_iota(jnp.int32, (width, base), 0) // CAP == core

    def body(i, kept):
        for j in range(BLOCK // 2):
            freq = i * (BLOCK // 2) + j
            sums = []
            for side, fac_ref in enumerate((own_ref, other_ref)):
                re = jnp.zeros((width, base), F32)
                im = jnp.zeros((width, base), F32)
                lane = 2 * j + side
                for pair in range(K // 2):
                    fac_re = fac_ref[freq, pl.ds(pair * 8, 8)].astype(F32)
                    fac_im = fac_ref[freq, pl.ds(16 + pair * 8, 8)].astype(F32)
                    kept_re = kept[pair * 8 : pair * 8 + 8, lane : lane + 1]
                    kept_im = kept[16 + pair * 8 : 24 + pair * 8, lane : lane + 1]
                    re = re + (fac_re * kept_re - fac_im * kept_im)
                    im = im + (fac_re * kept_im + fac_im * kept_re)
                sums.append((re + pltpu.roll(re, CAP, 0), im + pltpu.roll(im, CAP, 0)))
            for part in range(2):
                out_ref[freq, part] = jnp.where(mine, sums[0][part], sums[1][part]).astype(BF16)
        return pltpu.roll(kept, pairs - BLOCK, 1)

    lax.fori_loop(0, pairs // BLOCK, body, kept)


def final_kernel(target_ref, slots_ref, out_hbm, out_ref, sems):
    chips, _, width, base = slots_ref.shape
    rows = lax.broadcasted_iota(jnp.int32, (chips * width, MM), 0)
    placing = jnp.where(rows == target_ref[...], 1.0, 0.0).astype(BF16)
    copies = []
    for part in range(2):
        slots = slots_ref[:, part].reshape(chips * width, base)
        out_ref[part] = lax.dot_general(
            slots, placing, (((0,), (0,)), ((), ())), preferred_element_type=F32
        ).astype(BF16)
        copies.append(pltpu.make_async_copy(out_ref.at[part], out_hbm.at[part], sems.at[part]))
        copies[part].start()
    for copy in copies:
        copy.wait()


def local(vis_time, owner, counts, factors):
    n_chip = lax.axis_size("chip")
    n_freq = n_chip * lax.axis_size("core")
    n_bl = lax.axis_size("bl")
    chip, core = lax.axis_index("chip"), lax.axis_index("core")
    base = vis_time.shape[2]
    flat = vis_time.reshape(2 * base, NT)
    owner_row = owner.reshape(1, MM)
    width = 2 * CAP
    hbm = pl.BlockSpec(memory_space=pltpu.HBM)
    vmem = pl.BlockSpec(memory_space=pltpu.VMEM)
    smem = pl.BlockSpec(memory_space=pltpu.SMEM)
    wave = jnp.asarray(wave_half())
    outgoing, target = pl.pallas_call(
        dft_kernel,
        in_specs=[hbm, hbm, hbm],
        out_specs=[hbm, vmem],
        out_shape=[
            jax.ShapeDtypeStruct((n_chip, 2, width, base), BF16),
            jax.ShapeDtypeStruct((1, MM), jnp.int32),
        ],
        scratch_shapes=[
            pltpu.VMEM((1, MM), jnp.int32),
            pltpu.VMEM((4, 2 * base, CHUNK), BF16),
            pltpu.VMEM((2, CHUNK, 2 * MM), BF16),
            pltpu.VMEM((n_chip, 2, width, base), BF16),
            pltpu.SemaphoreType.DMA((9,)),
        ],
        compiler_params=pltpu.CompilerParams(vmem_limit_bytes=24 << 20),
        name="dft",
    )(*(pltpu.with_memory_space_constraint(a, pltpu.HBM) for a in (owner_row, flat, wave)))
    def exchange(rows):
        return lax.all_to_all(rows, "chip", split_axis=0, concat_axis=0, tiled=True)

    incoming = exchange(outgoing)

    factors, _ = lax.optimization_barrier((factors, outgoing))
    core_word = core.reshape(1)
    own, sent = pl.pallas_call(
        relay_kernel,
        grid=(4,),
        in_specs=[smem, pl.BlockSpec((CAP, n_freq // 4, 2, K, base), lambda i: (0, i, 0, 0, 0))],
        out_specs=[pl.BlockSpec((n_chip // 4, 2 * K * CAP, base), lambda i: (i, 0, 0))] * 2,
        out_shape=[jax.ShapeDtypeStruct((n_chip, 2 * K * CAP, base), BF16)] * 2,
        scratch_shapes=[pltpu.VMEM((base // 128, 2 * K * CAP + 8, 128), F32)],
        compiler_params=pltpu.CompilerParams(vmem_limit_bytes=8 << 20),
        name="relay",
    )(core_word, pltpu.with_memory_space_constraint(factors, pltpu.HBM))
    other = lax.ppermute(sent, "core", [(0, 1), (1, 0)])

    side = jnp.arange(2, dtype=jnp.int32)[:, None]
    slot_rows = (2 * chip + (core ^ side)) * CAP + jnp.arange(CAP, dtype=jnp.int32)
    mine = (target == slot_rows.reshape(2 * CAP, 1)).astype(BF16)
    limits = jnp.dot(mine, counts.astype(BF16), preferred_element_type=F32)
    lane = jnp.arange(n_freq, dtype=jnp.int32)
    chosen = (lane[:, None] == (lane & -2) + core).astype(BF16)
    limits = jnp.dot(limits.astype(BF16), chosen, preferred_element_type=F32)
    limits = jnp.where(lane & 1 == 0, limits[:CAP], limits[CAP:])

    partial, keep = pl.pallas_call(
        coef_kernel,
        in_specs=[smem, vmem, vmem, vmem, vmem],
        out_shape=[
            jax.ShapeDtypeStruct((n_bl, 2 * K * CAP, n_freq), F32),
            jax.ShapeDtypeStruct((2 * K * CAP, n_freq), F32),
        ],
        compiler_params=pltpu.CompilerParams(vmem_limit_bytes=8 << 20),
        name="coef",
    )(core_word, incoming, own, other, limits)
    partials = lax.all_to_all(partial, "bl", split_axis=0, concat_axis=0, tiled=True)
    synthesis = pl.pallas_call(
        synth_kernel,
        in_specs=[smem, vmem, vmem, vmem, vmem],
        out_shape=jax.ShapeDtypeStruct((n_chip, 2, width, base), BF16),
        compiler_params=pltpu.CompilerParams(vmem_limit_bytes=8 << 20),
        name="synth",
    )(core_word, partials, keep, own, other)
    returned = exchange(synthesis)
    filtered = pl.pallas_call(
        final_kernel,
        out_specs=hbm,
        out_shape=jax.ShapeDtypeStruct((2, base, MM), BF16),
        scratch_shapes=[pltpu.VMEM((2, base, MM), BF16), pltpu.SemaphoreType.DMA((2,))],
        compiler_params=pltpu.CompilerParams(vmem_limit_bytes=16 << 20),
        name="final",
    )(target, returned)
    return filtered[None]


def solution(mesh):
    n_freq, n_bl = mesh.devices.shape
    by_chip = jax.sharding.Mesh(
        mesh.devices.reshape(n_freq // 2, 2, n_bl), ("chip", "core", "bl")
    )
    freq = ("chip", "core")
    placed = (P(freq, None, "bl", None), P(), P(), P(freq, None, None, None, "bl"))
    return jax.shard_map(
        local, mesh=by_chip, in_specs=placed, out_specs=P(freq, None, "bl", None), check_vma=False
    )
```

```python
import math

import jax
import jax.numpy as jnp
import numpy as np
from jax import lax
from jax.experimental import pallas as pl
from jax.experimental.pallas import tpu as pltpu
from jax.sharding import PartitionSpec as P

NB = 1024
NT = 2048
K = 4
MM = 384
CAP = 4
CHUNK = NT // 4
BLOCK = 128
F32 = jnp.float32
BF16 = jnp.bfloat16


def wave_half():
    phases = np.outer(np.arange(NT // 2), np.arange(MM)) % NT
    angles = phases * (2.0 * math.pi / NT)
    rows = np.concatenate([np.cos(angles), np.sin(angles)], axis=1) / math.sqrt(NT)
    return rows.astype(np.float32).astype(jnp.bfloat16)


def dft_kernel(
    owner_hbm, vis_hbm, wave_hbm, out_hbm, target_ref, owner_ref, vis_ref, wave_ref, out_ref, sems
):
    chips, _, width, base = out_ref.shape
    owners = chips * width // CAP
    owner_copy = pltpu.make_async_copy(owner_hbm, owner_ref, sems.at[0])
    owner_copy.start()
    wave_copies, vis_copies = [], {}
    for part in range(2):
        wave_copies.append(
            pltpu.make_async_copy(
                wave_hbm.at[pl.ds(part * CHUNK, CHUNK)], wave_ref.at[part], sems.at[1 + part]
            )
        )
        wave_copies[-1].start()
        for chunk in (part, part + 2):
            vis_copies[chunk] = pltpu.make_async_copy(
                vis_hbm.at[:, pl.ds(chunk * CHUNK, CHUNK)], vis_ref.at[chunk], sems.at[3 + chunk]
            )
            vis_copies[chunk].start()
    owner_copy.wait()
    owner = owner_ref[...]
    hot = owner == lax.broadcasted_iota(jnp.int32, (owners, MM), 0)
    hot = jnp.where(hot, 1.0, 0.0)
    earlier = lax.broadcasted_iota(jnp.int32, (MM, MM), 0) < lax.broadcasted_iota(
        jnp.int32, (MM, MM), 1
    )
    earlier = jnp.where(earlier, 1.0, 0.0).astype(BF16)
    before = jnp.dot(hot.astype(BF16), earlier, preferred_element_type=F32)
    rank = jnp.sum(before * hot, axis=0, keepdims=True).astype(jnp.int32)
    target = owner * CAP + rank
    target_ref[...] = target
    rows = lax.broadcasted_iota(jnp.int32, (owners * CAP, MM), 0)
    placing = jnp.where(rows == target, 1.0, 0.0).astype(BF16)

    sign = 1 - 2 * (lax.broadcasted_iota(jnp.int32, (1, 2 * MM), 1) % 2)
    sign = sign.astype(F32)
    spectra = None
    for part in range(2):
        wave_copies[part].wait()
        for half in range(2):
            chunk = part + 2 * half
            vis_copies[chunk].wait()
            product = jnp.dot(vis_ref[chunk], wave_ref[part], preferred_element_type=F32)
            if half == 1:
                product = product * sign
            spectra = product if spectra is None else spectra + product
    real = spectra[:base, :MM] + spectra[base:, MM:]
    imag = spectra[base:, :MM] - spectra[:base, MM:]
    out_copies = []
    for part, modes in enumerate((real, imag)):
        placed = lax.dot_general(
            placing, modes.astype(BF16), (((1,), (1,)), ((), ())), preferred_element_type=F32
        )
        out_ref[:, part] = placed.astype(BF16).reshape(chips, width, base)
        out_copies.append(
            pltpu.make_async_copy(out_ref.at[:, part], out_hbm.at[:, part], sems.at[7 + part])
        )
        out_copies[part].start()
    for copy in out_copies:
        copy.wait()


def relay_kernel(core_ref, fac_ref, own_ref, sent_ref, rows_ref):
    core = core_ref[0]

    def body(i, carry):
        for out_ref, side in ((own_ref, core), (sent_ref, 1 - core)):
            for lane in range(rows_ref.shape[0]):
                for part in range(2):
                    for slot in range(CAP):
                        rows = fac_ref[slot, 2 * i + side, part, :, pl.ds(lane * 128, 128)]
                        first = part * K * CAP + slot
                        rows_ref[lane, pl.ds(first, K, stride=CAP), :] = rows.astype(F32)
                out_ref[i, :, pl.ds(lane * 128, 128)] = rows_ref[lane, : out_ref.shape[1]].astype(BF16)
        return carry

    lax.fori_loop(0, own_ref.shape[0], body, 0, unroll=4)


def coef_kernel(core_ref, vis_ref, own_ref, other_ref, limit_ref, out_ref, keep_ref):
    core = core_ref[0]
    chips, _, width, base = vis_ref.shape
    pairs = 2 * chips
    mine = lax.broadcasted_iota(jnp.int32, (width, base), 0) // CAP == core
    lanes = lax.broadcasted_iota(jnp.int32, (width, pairs), 1)
    ranks = lax.broadcasted_iota(jnp.int32, (2 * K * CAP, pairs), 0) // CAP % K
    limits = jnp.concatenate([limit_ref[...]] * (2 * K), axis=0)
    keep_ref[...] = jnp.where(ranks.astype(F32) < limits, 1.0, 0.0)

    def body(i, acc):
        acc = list(acc)
        for j in range(BLOCK // 2):
            freq = i * (BLOCK // 2) + j
            vis = [vis_ref[freq, part].astype(F32) for part in range(2)]
            swapped = [pltpu.roll(v, CAP, 0) for v in vis]
            for side, fac_ref in enumerate((own_ref, other_ref)):
                first, second = (vis, swapped) if side == 0 else (swapped, vis)
                vis_re = jnp.where(mine, first[0], second[0])
                vis_im = jnp.where(mine, first[1], second[1])
                here = lanes == 2 * freq + side
                for pair in range(K // 2):
                    fac_re = fac_ref[freq, pl.ds(pair * 8, 8)].astype(F32)
                    fac_im = fac_ref[freq, pl.ds(16 + pair * 8, 8)].astype(F32)
                    re = jnp.sum(fac_re * vis_re + fac_im * vis_im, axis=1, keepdims=True)
                    im = jnp.sum(fac_re * vis_im - fac_im * vis_re, axis=1, keepdims=True)
                    acc[pair] = jnp.where(here, re, acc[pair])
                    acc[2 + pair] = jnp.where(here, im, acc[2 + pair])
        return tuple(acc)

    zero = jnp.zeros((width, pairs), F32)
    acc = lax.fori_loop(0, pairs // BLOCK, body, (zero,) * 4)
    for at in range(4):
        for copy in range(out_ref.shape[0]):
            out_ref[copy, pl.ds(at * 8, 8), :] = acc[at]


def synth_kernel(core_ref, part_ref, keep_ref, own_ref, other_ref, out_ref):
    core = core_ref[0]
    chips, _, width, base = out_ref.shape
    pairs = 2 * chips
    total = part_ref[0]
    for source in range(1, part_ref.shape[0]):
        total = total + part_ref[source]
    kept = jnp.where(keep_ref[...] > 0, total, 0.0).astype(BF16).astype(F32)
    kept = kept * math.sqrt(NB / K)
    mine = lax.broadcasted_iota(jnp.int32, (width, base), 0) // CAP == core

    def body(i, kept):
        for j in range(BLOCK // 2):
            freq = i * (BLOCK // 2) + j
            sums = []
            for side, fac_ref in enumerate((own_ref, other_ref)):
                re = jnp.zeros((width, base), F32)
                im = jnp.zeros((width, base), F32)
                lane = 2 * j + side
                for pair in range(K // 2):
                    fac_re = fac_ref[freq, pl.ds(pair * 8, 8)].astype(F32)
                    fac_im = fac_ref[freq, pl.ds(16 + pair * 8, 8)].astype(F32)
                    kept_re = kept[pair * 8 : pair * 8 + 8, lane : lane + 1]
                    kept_im = kept[16 + pair * 8 : 24 + pair * 8, lane : lane + 1]
                    re = re + (fac_re * kept_re - fac_im * kept_im)
                    im = im + (fac_re * kept_im + fac_im * kept_re)
                sums.append((re + pltpu.roll(re, CAP, 0), im + pltpu.roll(im, CAP, 0)))
            for part in range(2):
                out_ref[freq, part] = jnp.where(mine, sums[0][part], sums[1][part]).astype(BF16)
        return pltpu.roll(kept, pairs - BLOCK, 1)

    lax.fori_loop(0, pairs // BLOCK, body, kept)


def final_kernel(target_ref, slots_ref, out_hbm, out_ref, sems):
    chips, _, width, base = slots_ref.shape
    rows = lax.broadcasted_iota(jnp.int32, (chips * width, MM), 0)
    placing = jnp.where(rows == target_ref[...], 1.0, 0.0).astype(BF16)
    copies = []
    for part in range(2):
        slots = slots_ref[:, part].reshape(chips * width, base)
        out_ref[part] = lax.dot_general(
            slots, placing, (((0,), (0,)), ((), ())), preferred_element_type=F32
        ).astype(BF16)
        copies.append(pltpu.make_async_copy(out_ref.at[part], out_hbm.at[part], sems.at[part]))
        copies[part].start()
    for copy in copies:
        copy.wait()


def local(vis_time, owner, counts, factors):
    n_chip = lax.axis_size("chip")
    n_freq = n_chip * lax.axis_size("core")
    n_bl = lax.axis_size("bl")
    chip, core = lax.axis_index("chip"), lax.axis_index("core")
    base = vis_time.shape[2]
    flat = vis_time.reshape(2 * base, NT)
    owner_row = owner.reshape(1, MM)
    width = 2 * CAP
    hbm = pl.BlockSpec(memory_space=pltpu.HBM)
    vmem = pl.BlockSpec(memory_space=pltpu.VMEM)
    smem = pl.BlockSpec(memory_space=pltpu.SMEM)
    wave = jnp.asarray(wave_half())
    outgoing, target = pl.pallas_call(
        dft_kernel,
        in_specs=[hbm, hbm, hbm],
        out_specs=[hbm, vmem],
        out_shape=[
            jax.ShapeDtypeStruct((n_chip, 2, width, base), BF16),
            jax.ShapeDtypeStruct((1, MM), jnp.int32),
        ],
        scratch_shapes=[
            pltpu.VMEM((1, MM), jnp.int32),
            pltpu.VMEM((4, 2 * base, CHUNK), BF16),
            pltpu.VMEM((2, CHUNK, 2 * MM), BF16),
            pltpu.VMEM((n_chip, 2, width, base), BF16),
            pltpu.SemaphoreType.DMA((9,)),
        ],
        compiler_params=pltpu.CompilerParams(vmem_limit_bytes=24 << 20),
        name="dft",
    )(*(pltpu.with_memory_space_constraint(a, pltpu.HBM) for a in (owner_row, flat, wave)))
    def exchange(rows):
        return lax.all_to_all(rows, "chip", split_axis=0, concat_axis=0, tiled=True)

    incoming = exchange(outgoing)

    factors, _ = lax.optimization_barrier((factors, outgoing))
    core_word = core.reshape(1)
    own, sent = pl.pallas_call(
        relay_kernel,
        grid=(4,),
        in_specs=[smem, pl.BlockSpec((CAP, n_freq // 4, 2, K, base), lambda i: (0, i, 0, 0, 0))],
        out_specs=[pl.BlockSpec((n_chip // 4, 2 * K * CAP, base), lambda i: (i, 0, 0))] * 2,
        out_shape=[jax.ShapeDtypeStruct((n_chip, 2 * K * CAP, base), BF16)] * 2,
        scratch_shapes=[pltpu.VMEM((base // 128, 2 * K * CAP + 8, 128), F32)],
        compiler_params=pltpu.CompilerParams(vmem_limit_bytes=8 << 20),
        name="relay",
    )(core_word, pltpu.with_memory_space_constraint(factors, pltpu.HBM))
    other = lax.ppermute(sent, "core", [(0, 1), (1, 0)])

    side = jnp.arange(2, dtype=jnp.int32)[:, None]
    slot_rows = (2 * chip + (core ^ side)) * CAP + jnp.arange(CAP, dtype=jnp.int32)
    mine = (target == slot_rows.reshape(2 * CAP, 1)).astype(BF16)
    limits = jnp.dot(mine, counts.astype(BF16), preferred_element_type=F32)
    lane = jnp.arange(n_freq, dtype=jnp.int32)
    chosen = (lane[:, None] == (lane & -2) + core).astype(BF16)
    limits = jnp.dot(limits.astype(BF16), chosen, preferred_element_type=F32)
    limits = jnp.where(lane & 1 == 0, limits[:CAP], limits[CAP:])

    partial, keep = pl.pallas_call(
        coef_kernel,
        in_specs=[smem, vmem, vmem, vmem, vmem],
        out_shape=[
            jax.ShapeDtypeStruct((n_bl, 2 * K * CAP, n_freq), F32),
            jax.ShapeDtypeStruct((2 * K * CAP, n_freq), F32),
        ],
        compiler_params=pltpu.CompilerParams(vmem_limit_bytes=8 << 20),
        name="coef",
    )(core_word, incoming, own, other, limits)
    partials = lax.all_to_all(partial, "bl", split_axis=0, concat_axis=0, tiled=True)
    synthesis = pl.pallas_call(
        synth_kernel,
        in_specs=[smem, vmem, vmem, vmem, vmem],
        out_shape=jax.ShapeDtypeStruct((n_chip, 2, width, base), BF16),
        compiler_params=pltpu.CompilerParams(vmem_limit_bytes=8 << 20),
        name="synth",
    )(core_word, partials, keep, own, other)
    returned = exchange(synthesis)
    filtered = pl.pallas_call(
        final_kernel,
        out_specs=hbm,
        out_shape=jax.ShapeDtypeStruct((2, base, MM), BF16),
        scratch_shapes=[pltpu.VMEM((2, base, MM), BF16), pltpu.SemaphoreType.DMA((2,))],
        compiler_params=pltpu.CompilerParams(vmem_limit_bytes=16 << 20),
        name="final",
    )(target, returned)
    return filtered[None]


def solution(mesh):
    n_freq, n_bl = mesh.devices.shape
    by_chip = jax.sharding.Mesh(
        mesh.devices.reshape(n_freq // 2, 2, n_bl), ("chip", "core", "bl")
    )
    freq = ("chip", "core")
    placed = (P(freq, None, "bl", None), P(), P(), P(freq, None, None, None, "bl"))
    return jax.shard_map(
        local, mesh=by_chip, in_specs=placed, out_specs=P(freq, None, "bl", None), check_vma=False
    )
```

```python
import math

import jax
import jax.numpy as jnp
import numpy as np
from jax import lax
from jax.experimental import pallas as pl
from jax.experimental.pallas import tpu as pltpu
from jax.sharding import PartitionSpec as P

NB = 1024
NT = 2048
K = 4
MM = 384
CAP = 4
CHUNK = NT // 4
BLOCK = 128
F32 = jnp.float32
BF16 = jnp.bfloat16


def wave_half():
    phases = np.outer(np.arange(NT // 2), np.arange(MM)) % NT
    angles = phases * (2.0 * math.pi / NT)
    rows = np.concatenate([np.cos(angles), np.sin(angles)], axis=1) / math.sqrt(NT)
    return rows.astype(np.float32).astype(jnp.bfloat16)


def dft_kernel(
    owner_hbm, vis_hbm, wave_hbm, out_hbm, target_ref, owner_ref, vis_ref, wave_ref, out_ref, sems
):
    chips, _, width, base = out_ref.shape
    owners = chips * width // CAP
    owner_copy = pltpu.make_async_copy(owner_hbm, owner_ref, sems.at[0])
    owner_copy.start()
    wave_copies, vis_copies = [], {}
    for part in range(2):
        wave_copies.append(
            pltpu.make_async_copy(
                wave_hbm.at[pl.ds(part * CHUNK, CHUNK)], wave_ref.at[part], sems.at[1 + part]
            )
        )
        wave_copies[-1].start()
        for chunk in (part, part + 2):
            vis_copies[chunk] = pltpu.make_async_copy(
                vis_hbm.at[:, pl.ds(chunk * CHUNK, CHUNK)], vis_ref.at[chunk], sems.at[3 + chunk]
            )
            vis_copies[chunk].start()
    owner_copy.wait()
    owner = owner_ref[...]
    hot = owner == lax.broadcasted_iota(jnp.int32, (owners, MM), 0)
    hot = jnp.where(hot, 1.0, 0.0)
    earlier = lax.broadcasted_iota(jnp.int32, (MM, MM), 0) < lax.broadcasted_iota(
        jnp.int32, (MM, MM), 1
    )
    earlier = jnp.where(earlier, 1.0, 0.0).astype(BF16)
    before = jnp.dot(hot.astype(BF16), earlier, preferred_element_type=F32)
    rank = jnp.sum(before * hot, axis=0, keepdims=True).astype(jnp.int32)
    target = owner * CAP + rank
    target_ref[...] = target
    rows = lax.broadcasted_iota(jnp.int32, (owners * CAP, MM), 0)
    placing = jnp.where(rows == target, 1.0, 0.0).astype(BF16)

    sign = 1 - 2 * (lax.broadcasted_iota(jnp.int32, (1, 2 * MM), 1) % 2)
    sign = sign.astype(F32)
    spectra = None
    for part in range(2):
        wave_copies[part].wait()
        for half in range(2):
            chunk = part + 2 * half
            vis_copies[chunk].wait()
            product = jnp.dot(vis_ref[chunk], wave_ref[part], preferred_element_type=F32)
            if half == 1:
                product = product * sign
            spectra = product if spectra is None else spectra + product
    real = spectra[:base, :MM] + spectra[base:, MM:]
    imag = spectra[base:, :MM] - spectra[:base, MM:]
    out_copies = []
    for part, modes in enumerate((real, imag)):
        placed = lax.dot_general(
            placing, modes.astype(BF16), (((1,), (1,)), ((), ())), preferred_element_type=F32
        )
        out_ref[:, part] = placed.astype(BF16).reshape(chips, width, base)
        out_copies.append(
            pltpu.make_async_copy(out_ref.at[:, part], out_hbm.at[:, part], sems.at[7 + part])
        )
        out_copies[part].start()
    for copy in out_copies:
        copy.wait()


def relay_kernel(core_ref, target_ref, fac_ref, own_ref, sent_ref, placing_ref, rows_ref):
    core = core_ref[0]
    rows = lax.broadcasted_iota(jnp.int32, placing_ref.shape, 0)
    rows = rows + pl.program_id(0) * placing_ref.shape[0]
    placing_ref[...] = jnp.where(rows == target_ref[...], 1.0, 0.0).astype(BF16)

    def body(i, carry):
        for out_ref, side in ((own_ref, core), (sent_ref, 1 - core)):
            for lane in range(rows_ref.shape[0]):
                for part in range(2):
                    for slot in range(CAP):
                        rows = fac_ref[slot, 2 * i + side, part, :, pl.ds(lane * 128, 128)]
                        first = part * K * CAP + slot
                        rows_ref[lane, pl.ds(first, K, stride=CAP), :] = rows.astype(F32)
                out_ref[i, :, pl.ds(lane * 128, 128)] = rows_ref[lane, : out_ref.shape[1]].astype(BF16)
        return carry

    lax.fori_loop(0, own_ref.shape[0], body, 0, unroll=4)


def coef_kernel(core_ref, vis_ref, own_ref, other_ref, limit_ref, out_ref, keep_ref):
    core = core_ref[0]
    chips, _, width, base = vis_ref.shape
    pairs = 2 * chips
    mine = lax.broadcasted_iota(jnp.int32, (width, base), 0) // CAP == core
    lanes = lax.broadcasted_iota(jnp.int32, (width, pairs), 1)
    ranks = lax.broadcasted_iota(jnp.int32, (2 * K * CAP, pairs), 0) // CAP % K
    limits = jnp.concatenate([limit_ref[...]] * (2 * K), axis=0)
    keep_ref[...] = jnp.where(ranks.astype(F32) < limits, 1.0, 0.0)

    def body(i, acc):
        acc = list(acc)
        for j in range(BLOCK // 2):
            freq = i * (BLOCK // 2) + j
            vis = [vis_ref[freq, part].astype(F32) for part in range(2)]
            swapped = [pltpu.roll(v, CAP, 0) for v in vis]
            for side, fac_ref in enumerate((own_ref, other_ref)):
                first, second = (vis, swapped) if side == 0 else (swapped, vis)
                vis_re = jnp.where(mine, first[0], second[0])
                vis_im = jnp.where(mine, first[1], second[1])
                here = lanes == 2 * freq + side
                for pair in range(K // 2):
                    fac_re = fac_ref[freq, pl.ds(pair * 8, 8)].astype(F32)
                    fac_im = fac_ref[freq, pl.ds(16 + pair * 8, 8)].astype(F32)
                    re = jnp.sum(fac_re * vis_re + fac_im * vis_im, axis=1, keepdims=True)
                    im = jnp.sum(fac_re * vis_im - fac_im * vis_re, axis=1, keepdims=True)
                    acc[pair] = jnp.where(here, re, acc[pair])
                    acc[2 + pair] = jnp.where(here, im, acc[2 + pair])
        return tuple(acc)

    zero = jnp.zeros((width, pairs), F32)
    acc = lax.fori_loop(0, pairs // BLOCK, body, (zero,) * 4)
    for at in range(4):
        for copy in range(out_ref.shape[0]):
            out_ref[copy, pl.ds(at * 8, 8), :] = acc[at]


def synth_kernel(core_ref, part_ref, keep_ref, own_ref, other_ref, out_ref):
    core = core_ref[0]
    chips, _, width, base = out_ref.shape
    pairs = 2 * chips
    total = part_ref[0]
    for source in range(1, part_ref.shape[0]):
        total = total + part_ref[source]
    kept = jnp.where(keep_ref[...] > 0, total, 0.0).astype(BF16).astype(F32)
    kept = kept * math.sqrt(NB / K)
    mine = lax.broadcasted_iota(jnp.int32, (width, base), 0) // CAP == core

    def body(i, kept):
        for j in range(BLOCK // 2):
            freq = i * (BLOCK // 2) + j
            sums = []
            for side, fac_ref in enumerate((own_ref, other_ref)):
                re = jnp.zeros((width, base), F32)
                im = jnp.zeros((width, base), F32)
                lane = 2 * j + side
                for pair in range(K // 2):
                    fac_re = fac_ref[freq, pl.ds(pair * 8, 8)].astype(F32)
                    fac_im = fac_ref[freq, pl.ds(16 + pair * 8, 8)].astype(F32)
                    kept_re = kept[pair * 8 : pair * 8 + 8, lane : lane + 1]
                    kept_im = kept[16 + pair * 8 : 24 + pair * 8, lane : lane + 1]
                    re = re + (fac_re * kept_re - fac_im * kept_im)
                    im = im + (fac_re * kept_im + fac_im * kept_re)
                sums.append((re + pltpu.roll(re, CAP, 0), im + pltpu.roll(im, CAP, 0)))
            for part in range(2):
                out_ref[freq, part] = jnp.where(mine, sums[0][part], sums[1][part]).astype(BF16)
        return pltpu.roll(kept, pairs - BLOCK, 1)

    lax.fori_loop(0, pairs // BLOCK, body, kept)


def final_kernel(placing_ref, slots_ref, out_hbm, out_ref, sems):
    chips, _, width, base = slots_ref.shape
    placing = placing_ref[...]
    copies = []
    for part in range(2):
        slots = slots_ref[:, part].reshape(chips * width, base)
        out_ref[part] = lax.dot_general(
            slots, placing, (((0,), (0,)), ((), ())), preferred_element_type=F32
        ).astype(BF16)
        copies.append(pltpu.make_async_copy(out_ref.at[part], out_hbm.at[part], sems.at[part]))
        copies[part].start()
    for copy in copies:
        copy.wait()


def local(vis_time, owner, counts, factors):
    n_chip = lax.axis_size("chip")
    n_freq = n_chip * lax.axis_size("core")
    n_bl = lax.axis_size("bl")
    chip, core = lax.axis_index("chip"), lax.axis_index("core")
    base = vis_time.shape[2]
    flat = vis_time.reshape(2 * base, NT)
    owner_row = owner.reshape(1, MM)
    width = 2 * CAP
    hbm = pl.BlockSpec(memory_space=pltpu.HBM)
    vmem = pl.BlockSpec(memory_space=pltpu.VMEM)
    smem = pl.BlockSpec(memory_space=pltpu.SMEM)
    wave = jnp.asarray(wave_half())
    outgoing, target = pl.pallas_call(
        dft_kernel,
        in_specs=[hbm, hbm, hbm],
        out_specs=[hbm, vmem],
        out_shape=[
            jax.ShapeDtypeStruct((n_chip, 2, width, base), BF16),
            jax.ShapeDtypeStruct((1, MM), jnp.int32),
        ],
        scratch_shapes=[
            pltpu.VMEM((1, MM), jnp.int32),
            pltpu.VMEM((4, 2 * base, CHUNK), BF16),
            pltpu.VMEM((2, CHUNK, 2 * MM), BF16),
            pltpu.VMEM((n_chip, 2, width, base), BF16),
            pltpu.SemaphoreType.DMA((9,)),
        ],
        compiler_params=pltpu.CompilerParams(vmem_limit_bytes=24 << 20),
        name="dft",
    )(*(pltpu.with_memory_space_constraint(a, pltpu.HBM) for a in (owner_row, flat, wave)))
    def exchange(rows):
        return lax.all_to_all(rows, "chip", split_axis=0, concat_axis=0, tiled=True)

    incoming = exchange(outgoing)

    factors, _ = lax.optimization_barrier((factors, outgoing))
    core_word = core.reshape(1)
    own, sent, placing = pl.pallas_call(
        relay_kernel,
        grid=(4,),
        in_specs=[
            smem,
            pl.BlockSpec((1, MM), lambda i: (0, 0)),
            pl.BlockSpec((CAP, n_freq // 4, 2, K, base), lambda i: (0, i, 0, 0, 0)),
        ],
        out_specs=[pl.BlockSpec((n_chip // 4, 2 * K * CAP, base), lambda i: (i, 0, 0))] * 2
        + [pl.BlockSpec((n_freq * CAP // 4, MM), lambda i: (i, 0))],
        out_shape=[jax.ShapeDtypeStruct((n_chip, 2 * K * CAP, base), BF16)] * 2
        + [jax.ShapeDtypeStruct((n_freq * CAP, MM), BF16)],
        scratch_shapes=[pltpu.VMEM((base // 128, 2 * K * CAP + 8, 128), F32)],
        compiler_params=pltpu.CompilerParams(vmem_limit_bytes=8 << 20),
        name="relay",
    )(core_word, target, pltpu.with_memory_space_constraint(factors, pltpu.HBM))
    other = lax.ppermute(sent, "core", [(0, 1), (1, 0)])

    side = jnp.arange(2, dtype=jnp.int32)[:, None]
    slot_rows = (2 * chip + (core ^ side)) * CAP + jnp.arange(CAP, dtype=jnp.int32)
    mine = (target == slot_rows.reshape(2 * CAP, 1)).astype(BF16)
    limits = jnp.dot(mine, counts.astype(BF16), preferred_element_type=F32)
    lane = jnp.arange(n_freq, dtype=jnp.int32)
    chosen = (lane[:, None] == (lane & -2) + core).astype(BF16)
    limits = jnp.dot(limits.astype(BF16), chosen, preferred_element_type=F32)
    limits = jnp.where(lane & 1 == 0, limits[:CAP], limits[CAP:])

    partial, keep = pl.pallas_call(
        coef_kernel,
        in_specs=[smem, vmem, vmem, vmem, vmem],
        out_shape=[
            jax.ShapeDtypeStruct((n_bl, 2 * K * CAP, n_freq), F32),
            jax.ShapeDtypeStruct((2 * K * CAP, n_freq), F32),
        ],
        compiler_params=pltpu.CompilerParams(vmem_limit_bytes=8 << 20),
        name="coef",
    )(core_word, incoming, own, other, limits)
    partials = lax.all_to_all(partial, "bl", split_axis=0, concat_axis=0, tiled=True)
    synthesis = pl.pallas_call(
        synth_kernel,
        in_specs=[smem, vmem, vmem, vmem, vmem],
        out_shape=jax.ShapeDtypeStruct((n_chip, 2, width, base), BF16),
        compiler_params=pltpu.CompilerParams(vmem_limit_bytes=8 << 20),
        name="synth",
    )(core_word, partials, keep, own, other)
    returned = exchange(synthesis)
    filtered = pl.pallas_call(
        final_kernel,
        out_specs=hbm,
        out_shape=jax.ShapeDtypeStruct((2, base, MM), BF16),
        scratch_shapes=[pltpu.VMEM((2, base, MM), BF16), pltpu.SemaphoreType.DMA((2,))],
        compiler_params=pltpu.CompilerParams(vmem_limit_bytes=16 << 20),
        name="final",
    )(placing, returned)
    return filtered[None]


def solution(mesh):
    n_freq, n_bl = mesh.devices.shape
    by_chip = jax.sharding.Mesh(
        mesh.devices.reshape(n_freq // 2, 2, n_bl), ("chip", "core", "bl")
    )
    freq = ("chip", "core")
    placed = (P(freq, None, "bl", None), P(), P(), P(freq, None, None, None, "bl"))
    return jax.shard_map(
        local, mesh=by_chip, in_specs=placed, out_specs=P(freq, None, "bl", None), check_vma=False
    )
```

```python
import math

import jax
import jax.numpy as jnp
import numpy as np
from jax import lax
from jax.experimental import pallas as pl
from jax.experimental.pallas import tpu as pltpu
from jax.sharding import PartitionSpec as P

NB = 1024
NT = 2048
K = 4
MM = 384
CAP = 4
CHUNK = NT // 4
BLOCK = 128
F32 = jnp.float32
BF16 = jnp.bfloat16


def wave_half():
    phases = np.outer(np.arange(NT // 2), np.arange(MM)) % NT
    angles = phases * (2.0 * math.pi / NT)
    rows = np.concatenate([np.cos(angles), np.sin(angles)], axis=1) / math.sqrt(NT)
    return rows.astype(np.float32).astype(jnp.bfloat16)


def dft_kernel(
    owner_hbm, vis_hbm, wave_hbm, out_hbm, target_ref, owner_ref, vis_ref, wave_ref, out_ref, sems
):
    chips, _, width, base = out_ref.shape
    owners = chips * width // CAP
    owner_copy = pltpu.make_async_copy(owner_hbm, owner_ref, sems.at[0])
    owner_copy.start()
    wave_copies, vis_copies = [], {}
    for part in range(2):
        wave_copies.append(
            pltpu.make_async_copy(
                wave_hbm.at[pl.ds(part * CHUNK, CHUNK)], wave_ref.at[part], sems.at[1 + part]
            )
        )
        wave_copies[-1].start()
        for chunk in (part, part + 2):
            vis_copies[chunk] = pltpu.make_async_copy(
                vis_hbm.at[:, pl.ds(chunk * CHUNK, CHUNK)], vis_ref.at[chunk], sems.at[3 + chunk]
            )
            vis_copies[chunk].start()
    owner_copy.wait()
    owner = owner_ref[...]
    hot = owner == lax.broadcasted_iota(jnp.int32, (owners, MM), 0)
    hot = jnp.where(hot, 1.0, 0.0)
    earlier = lax.broadcasted_iota(jnp.int32, (MM, MM), 0) < lax.broadcasted_iota(
        jnp.int32, (MM, MM), 1
    )
    earlier = jnp.where(earlier, 1.0, 0.0).astype(BF16)
    before = jnp.dot(hot.astype(BF16), earlier, preferred_element_type=F32)
    rank = jnp.sum(before * hot, axis=0, keepdims=True).astype(jnp.int32)
    target = owner * CAP + rank
    target_ref[...] = target
    rows = lax.broadcasted_iota(jnp.int32, (owners * CAP, MM), 0)
    placing = jnp.where(rows == target, 1.0, 0.0).astype(BF16)

    sign = 1 - 2 * (lax.broadcasted_iota(jnp.int32, (1, 2 * MM), 1) % 2)
    sign = sign.astype(F32)
    spectra = None
    for part in range(2):
        wave_copies[part].wait()
        for half in range(2):
            chunk = part + 2 * half
            vis_copies[chunk].wait()
            product = jnp.dot(vis_ref[chunk], wave_ref[part], preferred_element_type=F32)
            if half == 1:
                product = product * sign
            spectra = product if spectra is None else spectra + product
    real = spectra[:base, :MM] + spectra[base:, MM:]
    imag = spectra[base:, :MM] - spectra[:base, MM:]
    out_copies = []
    for part, modes in enumerate((real, imag)):
        placed = lax.dot_general(
            placing, modes.astype(BF16), (((1,), (1,)), ((), ())), preferred_element_type=F32
        )
        out_ref[:, part] = placed.astype(BF16).reshape(chips, width, base)
        for half in range(2):
            some = pl.ds(half * (chips // 2), chips // 2)
            out_copies.append(
                pltpu.make_async_copy(
                    out_ref.at[some, part], out_hbm.at[some, part], sems.at[7 + 2 * part + half]
                )
            )
            out_copies[-1].start()
    for copy in out_copies:
        copy.wait()


def relay_kernel(core_ref, fac_ref, own_ref, sent_ref, rows_ref):
    core = core_ref[0]

    def body(i, carry):
        for out_ref, side in ((own_ref, core), (sent_ref, 1 - core)):
            for lane in range(rows_ref.shape[0]):
                for part in range(2):
                    for slot in range(CAP):
                        rows = fac_ref[slot, 2 * i + side, part, :, pl.ds(lane * 128, 128)]
                        first = part * K * CAP + slot
                        rows_ref[lane, pl.ds(first, K, stride=CAP), :] = rows.astype(F32)
                out_ref[i, :, pl.ds(lane * 128, 128)] = rows_ref[lane, : out_ref.shape[1]].astype(BF16)
        return carry

    lax.fori_loop(0, own_ref.shape[0], body, 0, unroll=4)


def coef_kernel(core_ref, vis_ref, own_ref, other_ref, limit_ref, out_ref, keep_ref):
    core = core_ref[0]
    chips, _, width, base = vis_ref.shape
    pairs = 2 * chips
    mine = lax.broadcasted_iota(jnp.int32, (width, base), 0) // CAP == core
    lanes = lax.broadcasted_iota(jnp.int32, (width, pairs), 1)
    ranks = lax.broadcasted_iota(jnp.int32, (2 * K * CAP, pairs), 0) // CAP % K
    limits = jnp.concatenate([limit_ref[...]] * (2 * K), axis=0)
    keep_ref[...] = jnp.where(ranks.astype(F32) < limits, 1.0, 0.0)

    def body(i, acc):
        acc = list(acc)
        for j in range(BLOCK // 2):
            freq = i * (BLOCK // 2) + j
            vis = [vis_ref[freq, part].astype(F32) for part in range(2)]
            swapped = [pltpu.roll(v, CAP, 0) for v in vis]
            for side, fac_ref in enumerate((own_ref, other_ref)):
                first, second = (vis, swapped) if side == 0 else (swapped, vis)
                vis_re = jnp.where(mine, first[0], second[0])
                vis_im = jnp.where(mine, first[1], second[1])
                here = lanes == 2 * freq + side
                for pair in range(K // 2):
                    fac_re = fac_ref[freq, pl.ds(pair * 8, 8)].astype(F32)
                    fac_im = fac_ref[freq, pl.ds(16 + pair * 8, 8)].astype(F32)
                    re = jnp.sum(fac_re * vis_re + fac_im * vis_im, axis=1, keepdims=True)
                    im = jnp.sum(fac_re * vis_im - fac_im * vis_re, axis=1, keepdims=True)
                    acc[pair] = jnp.where(here, re, acc[pair])
                    acc[2 + pair] = jnp.where(here, im, acc[2 + pair])
        return tuple(acc)

    zero = jnp.zeros((width, pairs), F32)
    acc = lax.fori_loop(0, pairs // BLOCK, body, (zero,) * 4)
    for at in range(4):
        for copy in range(out_ref.shape[0]):
            out_ref[copy, pl.ds(at * 8, 8), :] = acc[at]


def synth_kernel(core_ref, part_ref, keep_ref, own_ref, other_ref, out_ref):
    core = core_ref[0]
    chips, _, width, base = out_ref.shape
    pairs = 2 * chips
    total = part_ref[0]
    for source in range(1, part_ref.shape[0]):
        total = total + part_ref[source]
    kept = jnp.where(keep_ref[...] > 0, total, 0.0).astype(BF16).astype(F32)
    kept = kept * math.sqrt(NB / K)
    mine = lax.broadcasted_iota(jnp.int32, (width, base), 0) // CAP == core

    def body(i, kept):
        for j in range(BLOCK // 2):
            freq = i * (BLOCK // 2) + j
            sums = []
            for side, fac_ref in enumerate((own_ref, other_ref)):
                re = jnp.zeros((width, base), F32)
                im = jnp.zeros((width, base), F32)
                lane = 2 * j + side
                for pair in range(K // 2):
                    fac_re = fac_ref[freq, pl.ds(pair * 8, 8)].astype(F32)
                    fac_im = fac_ref[freq, pl.ds(16 + pair * 8, 8)].astype(F32)
                    kept_re = kept[pair * 8 : pair * 8 + 8, lane : lane + 1]
                    kept_im = kept[16 + pair * 8 : 24 + pair * 8, lane : lane + 1]
                    re = re + (fac_re * kept_re - fac_im * kept_im)
                    im = im + (fac_re * kept_im + fac_im * kept_re)
                sums.append((re + pltpu.roll(re, CAP, 0), im + pltpu.roll(im, CAP, 0)))
            for part in range(2):
                out_ref[freq, part] = jnp.where(mine, sums[0][part], sums[1][part]).astype(BF16)
        return pltpu.roll(kept, pairs - BLOCK, 1)

    lax.fori_loop(0, pairs // BLOCK, body, kept)


def final_kernel(target_ref, slots_ref, out_hbm, out_ref, sems):
    chips, _, width, base = slots_ref.shape
    rows = lax.broadcasted_iota(jnp.int32, (chips * width, MM), 0)
    placing = jnp.where(rows == target_ref[...], 1.0, 0.0).astype(BF16)
    copies = []
    for part in range(2):
        slots = slots_ref[:, part].reshape(chips * width, base)
        out_ref[part] = lax.dot_general(
            slots, placing, (((0,), (0,)), ((), ())), preferred_element_type=F32
        ).astype(BF16)
        copies.append(pltpu.make_async_copy(out_ref.at[part], out_hbm.at[part], sems.at[part]))
        copies[part].start()
    for copy in copies:
        copy.wait()


def local(vis_time, owner, counts, factors):
    n_chip = lax.axis_size("chip")
    n_freq = n_chip * lax.axis_size("core")
    n_bl = lax.axis_size("bl")
    chip, core = lax.axis_index("chip"), lax.axis_index("core")
    base = vis_time.shape[2]
    flat = vis_time.reshape(2 * base, NT)
    owner_row = owner.reshape(1, MM)
    width = 2 * CAP
    hbm = pl.BlockSpec(memory_space=pltpu.HBM)
    vmem = pl.BlockSpec(memory_space=pltpu.VMEM)
    smem = pl.BlockSpec(memory_space=pltpu.SMEM)
    wave = jnp.asarray(wave_half())
    outgoing, target = pl.pallas_call(
        dft_kernel,
        in_specs=[hbm, hbm, hbm],
        out_specs=[hbm, vmem],
        out_shape=[
            jax.ShapeDtypeStruct((n_chip, 2, width, base), BF16),
            jax.ShapeDtypeStruct((1, MM), jnp.int32),
        ],
        scratch_shapes=[
            pltpu.VMEM((1, MM), jnp.int32),
            pltpu.VMEM((4, 2 * base, CHUNK), BF16),
            pltpu.VMEM((2, CHUNK, 2 * MM), BF16),
            pltpu.VMEM((n_chip, 2, width, base), BF16),
            pltpu.SemaphoreType.DMA((11,)),
        ],
        compiler_params=pltpu.CompilerParams(vmem_limit_bytes=24 << 20),
        name="dft",
    )(*(pltpu.with_memory_space_constraint(a, pltpu.HBM) for a in (owner_row, flat, wave)))
    def exchange(rows):
        return lax.all_to_all(rows, "chip", split_axis=0, concat_axis=0, tiled=True)

    incoming = exchange(outgoing)

    factors, _ = lax.optimization_barrier((factors, outgoing))
    core_word = core.reshape(1)
    own, sent = pl.pallas_call(
        relay_kernel,
        grid=(4,),
        in_specs=[smem, pl.BlockSpec((CAP, n_freq // 4, 2, K, base), lambda i: (0, i, 0, 0, 0))],
        out_specs=[pl.BlockSpec((n_chip // 4, 2 * K * CAP, base), lambda i: (i, 0, 0))] * 2,
        out_shape=[jax.ShapeDtypeStruct((n_chip, 2 * K * CAP, base), BF16)] * 2,
        scratch_shapes=[pltpu.VMEM((base // 128, 2 * K * CAP + 8, 128), F32)],
        compiler_params=pltpu.CompilerParams(vmem_limit_bytes=8 << 20),
        name="relay",
    )(core_word, pltpu.with_memory_space_constraint(factors, pltpu.HBM))
    other = lax.ppermute(sent, "core", [(0, 1), (1, 0)])

    side = jnp.arange(2, dtype=jnp.int32)[:, None]
    slot_rows = (2 * chip + (core ^ side)) * CAP + jnp.arange(CAP, dtype=jnp.int32)
    mine = (target == slot_rows.reshape(2 * CAP, 1)).astype(BF16)
    limits = jnp.dot(mine, counts.astype(BF16), preferred_element_type=F32)
    lane = jnp.arange(n_freq, dtype=jnp.int32)
    chosen = (lane[:, None] == (lane & -2) + core).astype(BF16)
    limits = jnp.dot(limits.astype(BF16), chosen, preferred_element_type=F32)
    limits = jnp.where(lane & 1 == 0, limits[:CAP], limits[CAP:])

    partial, keep = pl.pallas_call(
        coef_kernel,
        in_specs=[smem, vmem, vmem, vmem, vmem],
        out_shape=[
            jax.ShapeDtypeStruct((n_bl, 2 * K * CAP, n_freq), F32),
            jax.ShapeDtypeStruct((2 * K * CAP, n_freq), F32),
        ],
        compiler_params=pltpu.CompilerParams(vmem_limit_bytes=8 << 20),
        name="coef",
    )(core_word, incoming, own, other, limits)
    partials = lax.all_to_all(partial, "bl", split_axis=0, concat_axis=0, tiled=True)
    synthesis = pl.pallas_call(
        synth_kernel,
        in_specs=[smem, vmem, vmem, vmem, vmem],
        out_shape=jax.ShapeDtypeStruct((n_chip, 2, width, base), BF16),
        compiler_params=pltpu.CompilerParams(vmem_limit_bytes=8 << 20),
        name="synth",
    )(core_word, partials, keep, own, other)
    returned = exchange(synthesis)
    filtered = pl.pallas_call(
        final_kernel,
        out_specs=hbm,
        out_shape=jax.ShapeDtypeStruct((2, base, MM), BF16),
        scratch_shapes=[pltpu.VMEM((2, base, MM), BF16), pltpu.SemaphoreType.DMA((2,))],
        compiler_params=pltpu.CompilerParams(vmem_limit_bytes=16 << 20),
        name="final",
    )(target, returned)
    return filtered[None]


def solution(mesh):
    n_freq, n_bl = mesh.devices.shape
    by_chip = jax.sharding.Mesh(
        mesh.devices.reshape(n_freq // 2, 2, n_bl), ("chip", "core", "bl")
    )
    freq = ("chip", "core")
    placed = (P(freq, None, "bl", None), P(), P(), P(freq, None, None, None, "bl"))
    return jax.shard_map(
        local, mesh=by_chip, in_specs=placed, out_specs=P(freq, None, "bl", None), check_vma=False
    )
```
